32 devices in a mesh: band: 4 (over y, core), comp: 8 (over z, x).
Axes of the slice: x: 2, y: 2, z: 4, core: 2. Of those that a mesh axis runs over, the one named last changes fastest.
Arguments:
- tracer_mass: float32 [192, 8, 64, 512], P('comp', None, 'band'), may hold values from -6 to 6
- layer_mass: float32 [8, 64, 512], P('comp', 'band'), may hold values from 0.3 to 1.7
- zonal_wind: float32 [8, 64, 512], P('comp', 'band'), may hold values from -4 to 4
- merid_wind: float32 [8, 64, 512], P('comp', 'band'), may hold values from -4 to 4
- group_counts: int32 [8], replicated, may hold values from 1 to 24, 96 in all
- limiter_flags: int32 [96], replicated, may hold values 0 or 1
Outputs:
- tracers_out: float32 [192, 8, 64, 512], P('comp', None, 'band')
- height_out: float32 [8, 64, 512], P('comp', 'band')
- zonal_out: float32 [8, 64, 512], P('comp', 'band')
- merid_out: float32 [8, 64, 512], P('comp', 'band')
The draws below stay inside these ranges and needn't reach their ends.
Inputs may be any that keep to these rules, and one draw needn't show every extreme that they name: Group g lists the tracers numbered from the sum of the earlier groups' counts on, in its first group_counts[g] slots; the counts sum to 96 and the largest is exactly 24.
All inputs are finite; a program needn't handle non-finite values.
Results may differ from the reference program's by a relative error of at most 0.0003.
Values sent between devices are 32-bit elements; how exact they have to be, the bound alone decides.
No kernel may reach another device: no remote copies, remote signals or barrier semaphores. Data moves between devices by JAX's collectives and lax.ppermute only.
A program may use at most 128 MiB of HBM per device.

```python
import math
import jax
import jax.numpy as jnp
import numpy as np
from jax import lax

L = 8
NX = 512
NTR = 96
SLOTS = 24
STEPS = 4
NY = 64
N_COMP = 8


def with_ends(entries, stream_key, least, high):
    longest = entries.shape.index(max(entries.shape))
    spots = []
    for shift in (0, 1):
        where = [jax.random.randint(jax.random.fold_in(stream_key, axis), (), 0, length) for axis, length in enumerate(entries.shape)]
        where[longest] = (where[longest] + shift) % entries.shape[longest]
        spots.append(tuple(where))
    return entries.at[spots[0]].set(least).at[spots[1]].set(high)


def block_scale(rng, dims, split, least, high):
    factor_of = 1.0
    for position, parts in split:
        draws = jax.random.uniform(jax.random.fold_in(jax.random.fold_in(rng, 6), position), (parts,), jnp.float32, least / len(split), high / len(split))
        factor_of = factor_of * jnp.repeat(jnp.exp(draws), dims[position] // parts).reshape((-1,) + (1,) * (len(dims) - 1 - position))
    return factor_of


def split_up(number_of, total, reach, lean):
    loads = [(1 << 20) // math.isqrt(rank ** lean) + 1 for rank in range(2, number_of + 1)]
    rest, given = total - reach - (number_of - 1), [1] * (number_of - 1)
    while rest > 0:
        free = [i for i in range(number_of - 1) if given[i] < reach]
        whole, budget = sum([loads[i] for i in free]), rest
        for i in free:
            extra = min(reach - given[i], max(1, budget * loads[i] // whole), rest)
            given[i] = given[i] + extra
            rest = rest - extra
    return np.array([reach] + given)


def ragged(key, count, total, limit, skew):
    if count == 2:
        one = jax.random.randint(key, (), max(1, total - limit), min(limit, total - 1) + 1)
        return jnp.stack([one, total - one])
    lengths = jnp.asarray(split_up(count, total, limit, skew), jnp.int32)
    pairs = (count - 1) // 2
    donor, sink = lengths[1:1 + 2 * pairs:2], lengths[2:2 + 2 * pairs:2]
    margin = jnp.minimum(donor - 1, limit - sink)
    passed = jax.random.randint(jax.random.fold_in(key, 1), (pairs,), 0, 1 << 20) % (margin + 1)
    lengths = lengths.at[1:1 + 2 * pairs:2].set(donor - passed).at[2:2 + 2 * pairs:2].set(sink + passed)
    return lengths[jax.random.permutation(jax.random.fold_in(key, 2), count)]


def gaussian(own_key, extent, deviation, limit, split=(), kind=jnp.bfloat16):
    drawn = deviation * jax.random.normal(own_key, extent, jnp.float32)
    if split:
        drawn = drawn * block_scale(own_key, extent, split, -0.22, 0.18)
    return jnp.clip(drawn, -limit, limit).astype(kind)


def setup_inputs(seed: int = 0) -> dict:
    key_list = jax.random.split(jax.random.key(seed), 7)
    tracer_mass = gaussian(key_list[0], (N_COMP * SLOTS, L, NY, NX), 1.0, 6.0, ((0, 8), (2, 4)), jnp.float32)
    layer_mass = jnp.clip(0.3 + 1.40000004 * jax.random.uniform(key_list[1], (L, NY, NX), jnp.float32) ** block_scale(key_list[1], (L, NY, NX), ((0, 8), (1, 4)), -0.2, 0.2), 0.3, 1.7)
    zonal_wind = gaussian(key_list[2], (L, NY, NX), 1.0, 4.0, ((0, 8), (1, 4)), jnp.float32)
    merid_wind = gaussian(key_list[3], (L, NY, NX), 1.0, 4.0, ((0, 8), (1, 4)), jnp.float32)
    group_counts = ragged(key_list[4], N_COMP, NTR, SLOTS, 2).astype(jnp.int32)
    limiter_flags = with_ends((jax.random.randint(key_list[5], (NTR,), 0, 2) < 1).astype(jnp.int32), jax.random.fold_in(key_list[5], 1), 0, 1)
    return dict(tracer_mass=tracer_mass, layer_mass=layer_mass, zonal_wind=zonal_wind, merid_wind=merid_wind, group_counts=group_counts, limiter_flags=limiter_flags)


time_step = 0.1
gravity = 0.25
coriolis = 0.5
mass_floor = 0.5


def face_value(left_out, left_in, right_in, right_out, limited):
    raw_face = (7.0 / 12.0) * (left_in + right_in) - (1.0 / 12.0) * (left_out + right_out)
    bounded = jnp.clip(raw_face, jnp.minimum(left_in, right_in), jnp.maximum(left_in, right_in))
    return jnp.where(limited > 0, bounded, raw_face)


def advance(height, zonal_now, merid_now, padded, first_row, total_rows):
    row_count = height.shape[1]
    pad_height, pad_merid, pad_geo = padded[0], padded[2], padded[3]
    flux_south = 0.25 * (pad_merid[:, :row_count + 1] + pad_merid[:, 1:]) * (pad_height[:, :row_count + 1] + pad_height[:, 1:])
    face_row = first_row + lax.broadcasted_iota(jnp.int32, flux_south.shape, 1)
    flux_south = jnp.where((face_row > 0) & (face_row < total_rows), flux_south, 0.0)
    flux_east = 0.25 * (zonal_now + jnp.roll(zonal_now, -1, 2)) * (height + jnp.roll(height, -1, 2))
    new_height = height - time_step * (flux_east - jnp.roll(flux_east, 1, 2) + flux_south[:, 1:] - flux_south[:, :row_count])
    geopot = pad_geo[:, 1:row_count + 1]
    slope_x = jnp.roll(geopot, -1, 2) - jnp.roll(geopot, 1, 2)
    slope_y = pad_geo[:, 2:] - pad_geo[:, :row_count]
    new_zonal = zonal_now + time_step * (coriolis * merid_now - 0.5 * slope_x)
    new_merid = merid_now - time_step * (coriolis * zonal_now + 0.5 * slope_y)
    return new_height, new_zonal, new_merid, flux_east, flux_south


def tracer_update(item_mass, padded_ratio, flux_east, flux_south, limited):
    row_count = item_mass.shape[1]
    mix_ratio = padded_ratio[:, 2:row_count + 2]
    east_face = face_value(jnp.roll(mix_ratio, 1, 2), mix_ratio, jnp.roll(mix_ratio, -1, 2), jnp.roll(mix_ratio, -2, 2), limited)
    east_term = flux_east * east_face
    south_face = face_value(padded_ratio[:, :row_count + 1], padded_ratio[:, 1:row_count + 2], padded_ratio[:, 2:row_count + 3], padded_ratio[:, 3:], limited)
    south_term = flux_south * south_face
    return item_mass - time_step * (east_term - jnp.roll(east_term, 1, 2) + south_term[:, 1:] - south_term[:, :row_count])


def reference(tracer_mass, layer_mass, zonal_wind, merid_wind, group_counts, limiter_flags):
    height, zonal_now, merid_now = layer_mass, zonal_wind, merid_wind
    total_rows = height.shape[1]
    heights, east_list, south_list = [], [], []
    for step_index in range(STEPS):
        geopot = gravity * jnp.cumsum(height[::-1], 0)[::-1]
        padded = jnp.pad(jnp.stack([height, zonal_now, merid_now, geopot]), ((0, 0), (0, 0), (1, 1), (0, 0)))
        stepped = advance(height, zonal_now, merid_now, padded, 0, total_rows)
        heights.append(height)
        east_list.append(stepped[3])
        south_list.append(stepped[4])
        height, zonal_now, merid_now = stepped[0], stepped[1], stepped[2]
    counts = group_counts.astype(jnp.int32)
    starts = (jnp.cumsum(counts) - counts).astype(jnp.int32)

    def one_slot(slot_index):
        group = slot_index // SLOTS
        within = slot_index % SLOTS
        tracer_id = jnp.minimum(starts[group] + within, NTR - 1)
        limited = limiter_flags[tracer_id]
        item_mass = tracer_mass[slot_index]
        for step_index in range(STEPS):
            mix_ratio = item_mass / jnp.maximum(heights[step_index], mass_floor)
            padded_ratio = jnp.pad(mix_ratio, ((0, 0), (2, 2), (0, 0)))
            item_mass = tracer_update(item_mass, padded_ratio, east_list[step_index], south_list[step_index], limited)
        return jnp.where(within < counts[group], item_mass, 0.0)

    tracers_out = lax.map(one_slot, jnp.arange(N_COMP * SLOTS, dtype=jnp.int32))
    return tracers_out, height, zonal_now, merid_now
```

```python
import functools

import jax
import jax.numpy as jnp
from jax import lax
from jax.experimental import pallas as pl
from jax.experimental.pallas import tpu as pltpu
from jax.sharding import PartitionSpec as P

STEPS = 4
HALO = 2 * STEPS

time_step = 0.1
gravity = 0.25
coriolis = 0.5
mass_floor = 0.5


def lane_roll(x, shift):
    return pltpu.roll(x, shift % x.shape[-1], x.ndim - 1)


def band_shift(block, offset):
    count = lax.axis_size("band")
    pairs = [(i, i + offset) for i in range(count) if 0 <= i + offset < count]
    return lax.ppermute(block, "band", pairs)


def face_value(left_out, left_in, right_in, right_out, limited):
    raw_face = 7.0 / 12.0 * (left_in + right_in) - 1.0 / 12.0 * (left_out + right_out)
    if limited:
        low = jnp.minimum(left_in, right_in)
        high = jnp.maximum(left_in, right_in)
        raw_face = jnp.minimum(jnp.maximum(raw_face, low), high)
    return raw_face


def dynamics_kernel(place, own, north, south, inv_ref, east_ref, south_ref,
                    h_out, u_out, v_out, h0, u0, v0, h1, u1, v1, geo):
    levels, _, rows, _ = own.shape
    halo = north.shape[2]
    total = rows + 2 * halo
    for field, dst in enumerate((h0, u0, v0)):
        for q in range(0, halo, 8):
            dst[q:q + 8] = jnp.swapaxes(north[:, field, q:q + 8], 0, 1)
            dst[halo + rows + q:halo + rows + q + 8] = jnp.swapaxes(south[:, field, q:q + 8], 0, 1)
        for q in range(0, rows, 8):
            dst[halo + q:halo + q + 8] = jnp.swapaxes(own[:, field, q:q + 8], 0, 1)
    first_face = place[1] - halo
    face_end = place[2]
    level = lax.broadcasted_iota(jnp.int32, (levels, own.shape[-1]), 0)
    src, dst = (h0, u0, v0), (h1, u1, v1)
    for step in range(STEPS):
        h, u, v = src
        lo, hi = step, total - step

        def column_sum(j, carry):
            acc = h[j]
            span = 1
            while span < levels:
                moved = pltpu.roll(acc, levels - span, 0)
                acc = acc + jnp.where(level < levels - span, moved, 0.0)
                span *= 2
            geo[j] = gravity * acc
            inv_ref[step, j] = 1.0 / jnp.maximum(h[j], mass_floor)
            return carry

        lax.fori_loop(lo, hi, column_sum, 0, unroll=4)

        def south_flux(j):
            face = first_face + j
            scale = jnp.where((face > 0) & (face < face_end), 0.25 * time_step, 0.0)
            return scale * (v[j - 1] + v[j]) * (h[j - 1] + h[j])

        def advance(j, flux_north):
            hj, uj, vj, gj = h[j], u[j], v[j], geo[j]
            flux = south_flux(j + 1)
            east = (0.25 * time_step) * (uj + lane_roll(uj, -1)) * (hj + lane_roll(hj, -1))
            east_ref[step, j] = east
            south_ref[step, j] = flux_north
            dst[0][j] = hj - ((east - lane_roll(east, 1)) + (flux - flux_north))
            slope_x = lane_roll(gj, -1) - lane_roll(gj, 1)
            slope_y = geo[j + 1] - geo[j - 1]
            dst[1][j] = uj + time_step * (coriolis * vj - 0.5 * slope_x)
            dst[2][j] = vj - time_step * (coriolis * uj + 0.5 * slope_y)
            return flux

        last = lax.fori_loop(lo + 1, hi - 1, advance, south_flux(lo + 1), unroll=3)
        south_ref[step, hi - 1] = last
        src, dst = dst, src
    block = h_out.shape[0]
    for k in range(block):
        for r in range(rows):
            for out, field in zip((h_out, u_out, v_out), src):
                out[k, pl.ds(r, 1), :] = field[halo + r, pl.ds(place[0] * block + k, 1), :]


def tracer_kernel(place, counts, flags, mass, north, south, inv_ref, east_ref, south_ref, *rest, first, blocks):
    out_ref, cur0, cur1 = rest[-3:]
    slot = pl.program_id(0) + first
    levels, rows, _ = mass.shape[1:]
    halo = north.shape[2]
    total = rows + 2 * halo
    group = place[0]
    start = jnp.int32(0)
    for g in range(counts.shape[0]):
        start = start + jnp.where(g < group, counts[g], 0)
    live = slot < counts[group]
    flag = flags[jnp.minimum(start + slot, flags.shape[0] - 1)]

    def run(limited):
        for q in range(0, halo, 8):
            cur0[q:q + 8] = jnp.swapaxes(north[0, :, q:q + 8], 0, 1)
            cur0[halo + rows + q:halo + rows + q + 8] = jnp.swapaxes(south[0, :, q:q + 8], 0, 1)
        for q in range(0, rows, 8):
            cur0[halo + q:halo + q + 8] = jnp.swapaxes(mass[0, :, q:q + 8], 0, 1)
        src, dst = cur0, cur1
        for step in range(STEPS):
            lo, hi = 2 * (step + 1), total - 2 * (step + 1)
            size = next(b for b in range(blocks, 0, -1) if (hi - lo) % b == 0)

            def ratio(j):
                return src[j] * inv_ref[step, j]

            def south_term(j, a, b, c, d):
                return south_ref[step, j] * face_value(a, b, c, d, limited)

            near = [ratio(lo - 2), ratio(lo - 1), ratio(lo), ratio(lo + 1)]
            term = south_term(lo, *near)

            def sweep(k, carry):
                j = lo + k * size
                ratios = list(carry[:3])
                masses = [src[j + b] for b in range(size + 2)]
                ratios += [masses[b] * inv_ref[step, j + b] for b in range(2, size + 2)]
                terms = [carry[3]]
                terms += [south_term(j + b + 1, *ratios[b:b + 4]) for b in range(size)]
                done = []
                for b in range(size):
                    r = ratios[b + 1]
                    east = east_ref[step, j + b] * face_value(
                        lane_roll(r, 1), r, lane_roll(r, -1), lane_roll(r, -2), limited)
                    done.append(masses[b] - ((east - lane_roll(east, 1)) + (terms[b + 1] - terms[b])))
                for b in range(size):
                    dst[j + b] = done[b]
                return (*ratios[size:size + 3], terms[size])

            lax.fori_loop(0, (hi - lo) // size, sweep, (*near[1:], term))
            src, dst = dst, src
        for q in range(0, rows, 8):
            out_ref[0, :, q:q + 8] = jnp.swapaxes(src[halo + q:halo + q + 8], 0, 1)

    @pl.when(live & (flag > 0))
    def _():
        run(True)

    @pl.when(live & (flag <= 0))
    def _():
        run(False)

    @pl.when(jnp.logical_not(live))
    def _():
        out_ref[...] = jnp.zeros_like(out_ref)


def whole_block(shape):
    return pl.BlockSpec(shape, lambda *_: (0,) * len(shape))


def run_dynamics(place, own, north, south, level_block):
    levels, _, rows, columns = own.shape
    total = rows + 2 * HALO
    flux = jax.ShapeDtypeStruct((STEPS, total, levels, columns), jnp.float32)
    state = jax.ShapeDtypeStruct((level_block, rows, columns), jnp.float32)
    return pl.pallas_call(
        dynamics_kernel,
        grid_spec=pltpu.PrefetchScalarGridSpec(
            num_scalar_prefetch=1,
            grid=(1,),
            in_specs=[whole_block(own.shape), whole_block(north.shape), whole_block(south.shape)],
            out_specs=[whole_block(flux.shape)] * 3 + [whole_block(state.shape)] * 3,
            scratch_shapes=[pltpu.VMEM((total, levels, columns), jnp.float32)] * 7,
        ),
        out_shape=[flux] * 3 + [state] * 3,
        compiler_params=pltpu.CompilerParams(vmem_limit_bytes=48 << 20),
        name="dynamics",
    )(place, own, north, south)


def run_tracers(place, counts, flags, mass, north, south, fluxes, first, count, earlier):
    slots, levels, rows, columns = mass.shape
    total = rows + 2 * HALO

    def slot_block(height, shift):
        return pl.BlockSpec((1, levels, height, columns), lambda i, *_: (i + shift, 0, 0, 0))

    in_specs = [slot_block(rows, first), slot_block(HALO, 0), slot_block(HALO, 0)]
    in_specs += [whole_block(f.shape) for f in fluxes]
    operands = [mass, north, south, *fluxes]
    aliases = {}
    if earlier is not None:
        aliases = {3 + len(operands): 0}
        in_specs.append(pl.BlockSpec(memory_space=pl.ANY))
        operands.append(earlier)
    return pl.pallas_call(
        functools.partial(tracer_kernel, first=first, blocks=7),
        grid_spec=pltpu.PrefetchScalarGridSpec(
            num_scalar_prefetch=3,
            grid=(count,),
            in_specs=in_specs,
            out_specs=slot_block(rows, first),
            scratch_shapes=[pltpu.VMEM((total, levels, columns), jnp.float32)] * 2,
        ),
        out_shape=jax.ShapeDtypeStruct(mass.shape, jnp.float32),
        input_output_aliases=aliases,
        compiler_params=pltpu.CompilerParams(vmem_limit_bytes=48 << 20),
        name="tracers",
    )(place, counts, flags, *operands)


def on_device(tracer_mass, layer_mass, zonal_wind, merid_wind, group_counts, limiter_flags):
    n_comp = lax.axis_size("comp")
    n_band = lax.axis_size("band")
    slots, levels, rows, columns = tracer_mass.shape
    level_block = layer_mass.shape[0]
    place = jnp.stack([
        lax.axis_index("comp"), lax.axis_index("band") * rows, jnp.int32(rows * n_band)
    ]).astype(jnp.int32)
    chunk = slots // 2
    halos = []
    for first in range(0, slots, chunk):
        part = tracer_mass[first:first + chunk]
        halos.append((
            band_shift(part[:, :, rows - HALO:], 1),
            band_shift(part[:, :, :HALO], -1),
        ))
    state = jnp.stack([layer_mass, zonal_wind, merid_wind], 1)
    copies = jnp.broadcast_to(state[None], (n_comp, *state.shape)).reshape(n_comp * level_block, *state.shape[1:])
    gathered = lax.all_to_all(copies, "comp", 0, 0, tiled=True)
    from_north = band_shift(gathered[:, :, rows - HALO:], 1)
    from_south = band_shift(gathered[:, :, :HALO], -1)
    *fluxes, height, zonal, merid = run_dynamics(place, gathered, from_north, from_south, level_block)
    tracers = None
    for index, (north, south) in enumerate(halos):
        tracers = run_tracers(place, group_counts, limiter_flags, tracer_mass, north, south,
                              fluxes, index * chunk, chunk, tracers)
    return tracers, height, zonal, merid


def solution(mesh):
    placed = (
        P("comp", None, "band", None),
        P("comp", "band", None),
        P("comp", "band", None),
        P("comp", "band", None),
        P(),
        P(),
    )
    return jax.shard_map(
        on_device,
        mesh=mesh,
        in_specs=placed,
        out_specs=placed[:4],
        check_vma=False,
    )
```

```python
import functools

import jax
import jax.numpy as jnp
from jax import lax
from jax.experimental import pallas as pl
from jax.experimental.pallas import tpu as pltpu
from jax.sharding import PartitionSpec as P

STEPS = 4
HALO = 2 * STEPS

time_step = 0.1
gravity = 0.25
coriolis = 0.5
mass_floor = 0.5


LANES = 128


def band_shift(block, offset):
    count = lax.axis_size("band")
    pairs = [(i, i + offset) for i in range(count) if 0 <= i + offset < count]
    return lax.ppermute(block, "band", pairs)


def lane_index(shape):
    return lax.broadcasted_iota(jnp.int32, shape, len(shape) - 1)


def swap_bits(tiles):
    tiles = list(tiles)
    lane = lane_index(tiles[0].shape)
    bit = 1
    while bit < len(tiles):
        keep = (lane & bit) == 0
        for a in range(len(tiles)):
            if not a & bit:
                b = a | bit
                first, second = tiles[a], tiles[b]
                axis = first.ndim - 1
                tiles[a] = jnp.where(keep, first, pltpu.roll(second, bit, axis))
                tiles[b] = jnp.where(keep, pltpu.roll(first, LANES - bit, axis), second)
        bit *= 2
    return tiles


def neighbour_lanes(shape, parts, offset):
    lane = lane_index(shape)
    run = LANES // parts
    place = run * (lane % parts) + lane // parts
    place = (place + offset + LANES) % LANES
    return (place % run) * parts + place // run


def take_lanes(tile, index):
    return jnp.take_along_axis(tile, index, axis=1, mode="promise_in_bounds")


def split_row(row):
    return [row[..., p * LANES:(p + 1) * LANES] for p in range(row.shape[-1] // LANES)]


def arrange_kernel(mass, top, bottom):
    rows = mass.shape[2]
    half = rows // 2
    for out, base in ((top, 0), (bottom, half)):
        for q in range(0, half, 8):
            block = jnp.swapaxes(mass[0, :, base + q:base + q + 8], 0, 1)
            tiles = swap_bits(split_row(block))
            for p, tile in enumerate(tiles):
                out[0, q:q + 8, p] = tile


def dynamics_kernel(place, own, north, south, inv_ref, east_ref, south_ref,
                    h_out, u_out, v_out, h0, u0, v0, h1, u1, v1, geo):
    levels, _, rows, columns = own.shape
    parts = columns // LANES
    halo = north.shape[2]
    total = rows + 2 * halo
    for field, dst in enumerate((h0, u0, v0)):
        for source, base in ((north, 0), (own, halo), (south, halo + rows)):
            for q in range(0, source.shape[2], 8):
                block = jnp.swapaxes(source[:, field, q:q + 8], 0, 1)
                for p, tile in enumerate(swap_bits(split_row(block))):
                    dst[base + q:base + q + 8, p] = tile
    first_face = place[1] - halo
    face_end = place[2]
    shape = (levels, LANES)
    ahead = neighbour_lanes(shape, parts, 1)
    behind = neighbour_lanes(shape, parts, -1)
    level = lax.broadcasted_iota(jnp.int32, shape, 0)
    src, dst = (h0, u0, v0), (h1, u1, v1)
    for step in range(STEPS):
        h, u, v = src
        lo, hi = step, total - step

        def column_sum(j, carry):
            for p in range(parts):
                hp = h[j, p]
                acc = hp
                span = 1
                while span < levels:
                    moved = pltpu.roll(acc, levels - span, 0)
                    acc = acc + jnp.where(level < levels - span, moved, 0.0)
                    span *= 2
                geo[j, p] = gravity * acc
                inv_ref[step, j, p] = (1.0 / 12.0) / jnp.maximum(hp, mass_floor)
            return carry

        lax.fori_loop(lo, hi, column_sum, 0, unroll=2)

        def south_flux(j):
            face = first_face + j
            scale = jnp.where((face > 0) & (face < face_end), 0.25 * time_step, 0.0)
            return [scale * (v[j - 1, p] + v[j, p]) * (h[j - 1, p] + h[j, p]) for p in range(parts)]

        def advance(j, flux_north):
            hj, uj, vj, gj = ([f[j, p] for p in range(parts)] for f in (h, u, v, geo))
            hj.append(take_lanes(hj[0], ahead))
            uj.append(take_lanes(uj[0], ahead))
            gj = [take_lanes(gj[-1], behind), *gj, take_lanes(gj[0], ahead)]
            flux = south_flux(j + 1)
            east = [(0.25 * time_step) * (uj[p] + uj[p + 1]) * (hj[p] + hj[p + 1]) for p in range(parts)]
            east = [take_lanes(east[-1], behind), *east]
            for p in range(parts):
                east_ref[step, j, p] = east[p + 1]
                south_ref[step, j, p] = flux_north[p]
                dst[0][j, p] = hj[p] - ((east[p + 1] - east[p]) + (flux[p] - flux_north[p]))
                slope_x = gj[p + 2] - gj[p]
                slope_y = geo[j + 1, p] - geo[j - 1, p]
                dst[1][j, p] = uj[p] + time_step * (coriolis * vj[p] - 0.5 * slope_x)
                dst[2][j, p] = vj[p] - time_step * (coriolis * uj[p] + 0.5 * slope_y)
            return flux

        last = lax.fori_loop(lo + 1, hi - 1, advance, south_flux(lo + 1), unroll=2)
        for p in range(parts):
            south_ref[step, hi - 1, p] = last[p]
        src, dst = dst, src
    block = h_out.shape[0]
    for out, field in zip((h_out, u_out, v_out), src):
        for k in range(block):
            mine = pl.ds(place[0] * block + k, 1)
            for r in range(rows):
                tiles = swap_bits([field[halo + r, p, mine, :] for p in range(parts)])
                for p, tile in enumerate(tiles):
                    out[k, r:r + 1, p * LANES:(p + 1) * LANES] = tile


def tracer_kernel(place, counts, flags, north, top, bottom, south, inv_ref, east_ref, south_ref, *rest, first, size):
    out_ref, cur, even, odd = rest[-4:]
    slot = pl.program_id(0) + first
    parts = north.shape[2]
    levels = north.shape[3]
    halo = north.shape[1]
    half = top.shape[1]
    rows = 2 * half
    total = rows + 2 * halo
    group = place[0]
    start = jnp.int32(0)
    for g in range(counts.shape[0]):
        start = start + jnp.where(g < group, counts[g], 0)
    live = slot < counts[group]
    flag = flags[jnp.minimum(start + slot, flags.shape[0] - 1)]
    shape = (levels, LANES)

    def run(limited):
        ahead = neighbour_lanes(shape, parts, 1)
        behind = neighbour_lanes(shape, parts, -1)

        def spread(buffer, j, tiles):
            for p in range(parts):
                buffer[j, p + 1] = tiles[p]
            buffer[j, 0] = take_lanes(tiles[-1], behind)
            buffer[j, parts + 1] = take_lanes(tiles[0], ahead)
            buffer[j, parts + 2] = take_lanes(tiles[1], ahead)

        for source, base in ((north, 0), (top, halo), (bottom, halo + half), (south, halo + rows)):
            def enter(r, carry):
                tiles = [source[0, r, p] for p in range(parts)]
                for p in range(parts):
                    cur[size + base + r, p] = tiles[p]
                spread(even, size + base + r, [tiles[p] * inv_ref[0, base + r, p] for p in range(parts)])
                return carry
            lax.fori_loop(0, source.shape[1], enter, 0, unroll=True)

        def face(a2, a, b, b2, bounds):
            raw = 7.0 * (a + b) - (a2 + b2)
            if limited:
                raw = jnp.minimum(jnp.maximum(raw, jnp.minimum(*bounds)), jnp.maximum(*bounds))
            return raw

        def scaled(tiles):
            return [12.0 * t for t in tiles] if limited else [None] * len(tiles)

        src, dst = even, odd
        for step in range(STEPS):
            lo, hi = 2 * (step + 1), total - 2 * (step + 1)
            onward = step + 1 < STEPS

            def south_terms(j, near, bounds):
                return [south_ref[step, j, p] * face(*(t[p] for t in near), tuple(t[p] for t in bounds))
                        for p in range(parts)]

            near = [[src[size + lo - 2 + b, p + 1] for p in range(parts)] for b in range(4)]
            term = south_terms(lo, near, [scaled(near[1]), scaled(near[2])])

            def finish(j, partial, moved):
                for b in range(size):
                    at = size + j - size + b
                    tiles = [partial[b] + moved[b]]
                    cur[at, 0] = tiles[0]
                    if onward:
                        tiles += [cur[at, p] for p in range(1, parts)]
                        factor = [inv_ref[step + 1, jnp.maximum(j - size + b, 0), p] for p in range(parts)]
                        spread(dst, at, [t * f for t, f in zip(tiles, factor)])

            def sweep(k, carry):
                term, partial, moved = carry
                j = lo + k * size
                table = [[src[size + j - 1 + b, p + 1] for p in range(parts)] for b in range(size + 3)]
                bounds = [None] + [scaled(t) for t in table[1:size + 2]]
                masses = [[cur[size + j + b, p] for p in range(parts)] for b in range(size)]
                next_partial, next_moved, stores = [], [], []
                for b in range(size):
                    at = size + j + b
                    wide = [src[at, 0], *table[b + 1], src[at, parts + 1], src[at, parts + 2]]
                    limit = bounds[b + 1] + scaled([wide[parts + 1]])
                    east = [east_ref[step, j + b, p] * face(*wide[p:p + 4], (limit[p], limit[p + 1]))
                            for p in range(parts)]
                    next_moved.append(take_lanes(east[-1], behind))
                    following = south_terms(j + b + 1, table[b:b + 4], bounds[b + 1:b + 3])
                    next_partial.append(masses[b][0] - (east[0] + (following[0] - term[0])))
                    stores.append([masses[b][p] - ((east[p] - east[p - 1]) + (following[p] - term[p]))
                                   for p in range(1, parts)])
                    term = following
                finish(j, partial, moved)
                for b in range(size):
                    for p in range(1, parts):
                        cur[size + j + b, p] = stores[b][p - 1]
                return term, next_partial, next_moved

            zeros = [jnp.zeros(shape, jnp.float32)] * size
            count = (hi - lo) // size
            term, partial, moved = lax.fori_loop(0, count, sweep, (term, zeros, zeros))
            finish(hi, partial, moved)
            src, dst = dst, src
        for q in range(0, rows, 8):
            base = size + halo + q
            tiles = swap_bits([cur[base:base + 8, p] for p in range(parts)])
            for p, tile in enumerate(tiles):
                out_ref[0, :, q:q + 8, p * LANES:(p + 1) * LANES] = jnp.swapaxes(tile, 0, 1)

    @pl.when(live & (flag > 0))
    def _():
        run(True)

    @pl.when(live & (flag <= 0))
    def _():
        run(False)

    @pl.when(jnp.logical_not(live))
    def _():
        out_ref[...] = jnp.zeros_like(out_ref)


def whole_block(shape):
    return pl.BlockSpec(shape, lambda *_: (0,) * len(shape))


def run_arrange(mass, first, count):
    _, levels, rows, columns = mass.shape
    half = jax.ShapeDtypeStruct((count, rows // 2, columns // LANES, levels, LANES), jnp.float32)
    return pl.pallas_call(
        arrange_kernel,
        grid=(count,),
        in_specs=[pl.BlockSpec((1, levels, rows, columns), lambda i: (i + first, 0, 0, 0))],
        out_specs=[pl.BlockSpec((1, *half.shape[1:]), lambda i: (i, 0, 0, 0, 0))] * 2,
        out_shape=[half] * 2,
        name="arrange",
    )(mass)


def run_dynamics(place, own, north, south, level_block):
    levels, _, rows, columns = own.shape
    total = rows + 2 * HALO
    tiles = (total, columns // LANES, levels, LANES)
    flux = jax.ShapeDtypeStruct((STEPS, *tiles), jnp.float32)
    state = jax.ShapeDtypeStruct((level_block, rows, columns), jnp.float32)
    return pl.pallas_call(
        dynamics_kernel,
        grid_spec=pltpu.PrefetchScalarGridSpec(
            num_scalar_prefetch=1,
            grid=(1,),
            in_specs=[whole_block(own.shape), whole_block(north.shape), whole_block(south.shape)],
            out_specs=[whole_block(flux.shape)] * 3 + [whole_block(state.shape)] * 3,
            scratch_shapes=[pltpu.VMEM(tiles, jnp.float32)] * 7,
        ),
        out_shape=[flux] * 3 + [state] * 3,
        compiler_params=pltpu.CompilerParams(vmem_limit_bytes=48 << 20),
        name="dynamics",
    )(place, own, north, south)


def run_tracers(place, counts, flags, blocks, fluxes, first, out_shape, earlier, size=4):
    count, half, parts, levels, lanes = blocks[0].shape
    total = 2 * half + 2 * HALO
    in_specs = [pl.BlockSpec((1, *b.shape[1:]), lambda i, *_: (i, 0, 0, 0, 0)) for b in blocks]
    in_specs += [whole_block(f.shape) for f in fluxes]
    operands = [*blocks, *fluxes]
    aliases = {}
    if earlier is not None:
        aliases = {3 + len(operands): 0}
        in_specs.append(pl.BlockSpec(memory_space=pl.ANY))
        operands.append(earlier)
    wide = pltpu.VMEM((total + size, parts + 3, levels, lanes), jnp.float32)
    return pl.pallas_call(
        functools.partial(tracer_kernel, first=first, size=size),
        grid_spec=pltpu.PrefetchScalarGridSpec(
            num_scalar_prefetch=3,
            grid=(count,),
            in_specs=in_specs,
            out_specs=pl.BlockSpec((1, *out_shape[1:]), lambda i, *_: (i + first, 0, 0, 0)),
            scratch_shapes=[pltpu.VMEM((total + size, parts, levels, lanes), jnp.float32), wide, wide],
        ),
        out_shape=jax.ShapeDtypeStruct(out_shape, jnp.float32),
        input_output_aliases=aliases,
        compiler_params=pltpu.CompilerParams(vmem_limit_bytes=48 << 20),
        name="tracers",
    )(place, counts, flags, *operands)


def on_device(tracer_mass, layer_mass, zonal_wind, merid_wind, group_counts, limiter_flags):
    n_comp = lax.axis_size("comp")
    n_band = lax.axis_size("band")
    slots, levels, rows, columns = tracer_mass.shape
    level_block = layer_mass.shape[0]
    assert rows == 2 * HALO and levels == 8
    place = jnp.stack([
        lax.axis_index("comp"), lax.axis_index("band") * rows, jnp.int32(rows * n_band)
    ]).astype(jnp.int32)
    state = jnp.stack([layer_mass, zonal_wind, merid_wind], 1)
    copies = jnp.broadcast_to(state[None], (n_comp, *state.shape)).reshape(n_comp * level_block, *state.shape[1:])
    gathered = lax.all_to_all(copies, "comp", 0, 0, tiled=True)
    chunk = slots // 2
    halves = [run_arrange(tracer_mass, first, chunk) for first in range(0, slots, chunk)]

    def exchange(top, bottom):
        return (band_shift(bottom, 1), top, bottom, band_shift(top, -1))

    blocks = [exchange(*halves[0])]
    from_north = band_shift(gathered[:, :, rows - HALO:], 1)
    from_south = band_shift(gathered[:, :, :HALO], -1)
    top, bottom, from_north, from_south = lax.optimization_barrier((*halves[1], from_north, from_south))
    blocks.append(exchange(top, bottom))
    *fluxes, height, zonal, merid = run_dynamics(place, gathered, from_north, from_south, level_block)
    tracers = None
    for index, block in enumerate(blocks):
        tracers = run_tracers(place, group_counts, limiter_flags, block, fluxes, index * chunk,
                              tracer_mass.shape, tracers)
    return tracers, height, zonal, merid


def solution(mesh):
    placed = (
        P("comp", None, "band", None),
        P("comp", "band", None),
        P("comp", "band", None),
        P("comp", "band", None),
        P(),
        P(),
    )
    return jax.shard_map(
        on_device,
        mesh=mesh,
        in_specs=placed,
        out_specs=placed[:4],
        check_vma=False,
    )
```

```python
import functools
import math

import jax
import jax.numpy as jnp
from jax import lax
from jax.experimental import pallas as pl
from jax.experimental.pallas import tpu as pltpu
from jax.sharding import PartitionSpec as P


STEPS = 4
HALO = 2 * STEPS

time_step = 0.1
gravity = 0.25
coriolis = 0.5
mass_floor = 0.5


LANES = 128
DELAY = 3


def band_shift(block, offset):
    count = lax.axis_size("band")
    pairs = [(i, i + offset) for i in range(count) if 0 <= i + offset < count]
    return lax.ppermute(block, "band", pairs)


def lane_index(shape):
    return lax.broadcasted_iota(jnp.int32, shape, len(shape) - 1)


def swap_bits(tiles):
    tiles = list(tiles)
    lane = lane_index(tiles[0].shape)
    bit = 1
    while bit < len(tiles):
        keep = (lane & bit) == 0
        for a in range(len(tiles)):
            if not a & bit:
                b = a | bit
                first, second = tiles[a], tiles[b]
                axis = first.ndim - 1
                tiles[a] = jnp.where(keep, first, pltpu.roll(second, bit, axis))
                tiles[b] = jnp.where(keep, pltpu.roll(first, LANES - bit, axis), second)
        bit *= 2
    return tiles


def lane_order(shape, parts, inverse):
    lane = lane_index(shape)
    few, many = (parts, LANES // parts) if inverse else (LANES // parts, parts)
    return (lane & (few - 1)) * many + (lane >> (few.bit_length() - 1))


def take_lanes(tile, index):
    return jnp.take_along_axis(tile, index, axis=1, mode="promise_in_bounds")


def interleave(tiles):
    order = lane_order(tiles[0].shape[-2:], len(tiles), False)
    return [take_each(t, order) for t in swap_bits(tiles)]


def restore(tiles):
    order = lane_order(tiles[0].shape[-2:], len(tiles), True)
    return swap_bits([take_each(t, order) for t in tiles])


def take_each(tile, order):
    if tile.ndim == 2:
        return take_lanes(tile, order)
    return jnp.stack([take_lanes(tile[i], order) for i in range(tile.shape[0])])


def after(tile):
    return pltpu.roll(tile, LANES - 1, 1)


def before(tile):
    return pltpu.roll(tile, 1, 1)


def plane_order(levels):
    majors = levels // 2
    swapped = [(field, d, flip) for flip in range(2) for d in range(majors) for field in (1, 2)]
    return swapped + [(0, d, flip) for d in range(majors) for flip in range(2)]


def source_level(comp, levels, major, flip):
    majors = levels // 2
    at = (comp >> 1) - major
    return jnp.where(at < 0, at + majors, at) * 2 + ((comp & 1) ^ flip)


def split_row(row):
    return [row[..., p * LANES:(p + 1) * LANES] for p in range(row.shape[-1] // LANES)]


def arrange_kernel(mass, top, bottom):
    rows = mass.shape[2]
    half = rows // 2

    def one(t, carry):
        for out, base in ((top, 0), (bottom, half)):
            for q in range(0, half, 8):
                block = jnp.swapaxes(mass[t, :, base + q:base + q + 8], 0, 1)
                for p, tile in enumerate(interleave(split_row(block))):
                    out[t, q:q + 8, p] = tile
        return carry

    lax.fori_loop(0, mass.shape[0], one, 0)


def dynamics_kernel(place, own, north, south, inv_ref, east_ref, south_ref,
                    h_out, u_out, v_out, h0, u0, v0, h1, u1, v1, geo, stage):
    planes, rows, columns = own.shape
    parts = columns // LANES
    halo = north.shape[1]
    total = rows + 2 * halo
    levels = planes // 3
    for plane, (field, major, flip) in enumerate(plane_order(levels)):
        level = source_level(place[0], levels, major, flip)
        for source, base in ((north, 0), (own, halo), (south, halo + rows)):
            stage[field, level, base:base + source.shape[1]] = source[plane]
    for field, dst in enumerate((h0, u0, v0)):
        for q in range(0, total, 8):
            block = jnp.swapaxes(stage[field, :, q:q + 8], 0, 1)
            for p, tile in enumerate(interleave(split_row(block))):
                dst[q:q + 8, p] = tile
    first_face = place[1] - halo
    scales = [jnp.where((first_face + j > 0) & (first_face + j < place[2]), 0.25 * time_step, 0.0)
              for j in range(total)]
    level = lax.broadcasted_iota(jnp.int32, (levels, LANES), 0)
    src, dst = (h0, u0, v0), (h1, u1, v1)
    for step in range(STEPS):
        h, u, v = src
        lo, hi = step, total - step
        for j in range(lo, hi):
            for p in range(parts):
                hp = h[j, p]
                acc = hp
                span = 1
                while span < levels:
                    moved = pltpu.roll(acc, levels - span, 0)
                    acc = acc + jnp.where(level < levels - span, moved, 0.0)
                    span *= 2
                geo[j, p] = gravity * acc
                inv_ref[step, j, p] = (1.0 / 12.0) / jnp.maximum(hp, mass_floor)

        def south_flux(j):
            return [scales[j] * (v[j - 1, p] + v[j, p]) * (h[j - 1, p] + h[j, p]) for p in range(parts)]

        def finish(j, tiles, moved):
            dst[0][j, 0] = tiles[0] + moved
            for p in range(1, parts):
                dst[0][j, p] = tiles[p]

        flux_north = south_flux(lo + 1)
        pending = []
        for j in range(lo + 1, hi - 1):
            hj, uj, vj, gj = ([f[j, p] for p in range(parts)] for f in (h, u, v, geo))
            hj.append(after(hj[0]))
            uj.append(after(uj[0]))
            gj = [before(gj[-1]), *gj, after(gj[0])]
            flux = south_flux(j + 1)
            east = [(0.25 * time_step) * (uj[p] + uj[p + 1]) * (hj[p] + hj[p + 1]) for p in range(parts)]
            tiles = [hj[0] - (east[0] + (flux[0] - flux_north[0]))]
            tiles += [hj[p] - ((east[p] - east[p - 1]) + (flux[p] - flux_north[p])) for p in range(1, parts)]
            pending.append((j, tiles, before(east[-1])))
            for p in range(parts):
                east_ref[step, j, p] = east[p]
                south_ref[step, j, p] = flux_north[p]
                slope_x = gj[p + 2] - gj[p]
                slope_y = geo[j + 1, p] - geo[j - 1, p]
                dst[1][j, p] = uj[p] + time_step * (coriolis * vj[p] - 0.5 * slope_x)
                dst[2][j, p] = vj[p] - time_step * (coriolis * uj[p] + 0.5 * slope_y)
            flux_north = flux
            if len(pending) > DELAY:
                finish(*pending.pop(0))
        for one in pending:
            finish(*one)
        for p in range(parts):
            south_ref[step, hi - 1, p] = flux_north[p]
        src, dst = dst, src
    block = h_out.shape[0]
    for out, field in zip((h_out, u_out, v_out), src):
        for k in range(block):
            mine = pl.ds(place[0] * block + k, 1)
            for q in range(0, rows, 8):
                tiles = restore([
                    jnp.concatenate([field[halo + q + i, p, mine, :] for i in range(8)], 0) for p in range(parts)])
                for p, tile in enumerate(tiles):
                    out[k, q:q + 8, p * LANES:(p + 1) * LANES] = tile


def tracer_kernel(place, counts, flags, north, top, bottom, south, inv_ref, east_ref, south_ref, *rest, first):
    out_ref, cur, even, odd = rest[-4:]
    slot = pl.program_id(0) + first
    parts = north.shape[2]
    halo = north.shape[1]
    half = top.shape[1]
    rows = 2 * half
    total = rows + 2 * halo
    group = place[0]
    start = jnp.int32(0)
    for g in range(counts.shape[0]):
        start = start + jnp.where(g < group, counts[g], 0)
    live = slot < counts[group]
    flag = flags[jnp.minimum(start + slot, flags.shape[0] - 1)]

    def entry(j):
        for source, base in ((south, halo + rows), (bottom, halo + half), (top, halo), (north, 0)):
            if j >= base:
                return [source[0, j - base, p] for p in range(parts)]

    def run(limited):
        def spread(buffer, j, tiles):
            for p in range(parts):
                buffer[j, p + 1] = tiles[p]
            buffer[j, 0] = before(tiles[-1])
            buffer[j, parts + 1] = after(tiles[0])
            buffer[j, parts + 2] = after(tiles[1])

        for j in range(total):
            spread(even, j, [t * inv_ref[0, j, p] for p, t in enumerate(entry(j))])

        def face(a2, a, b, b2, bounds):
            raw = 7.0 * (a + b) - (a2 + b2)
            if limited:
                raw = jnp.minimum(jnp.maximum(raw, jnp.minimum(*bounds)), jnp.maximum(*bounds))
            return raw

        def scaled(tiles):
            return [12.0 * t for t in tiles] if limited else [None] * len(tiles)

        src, dst = even, odd
        for step in range(STEPS):
            lo, hi = 2 * (step + 1), total - 2 * (step + 1)

            def south_terms(j, near, bounds):
                return [south_ref[step, j, p] * face(*(t[p] for t in near), tuple(t[p] for t in bounds))
                        for p in range(parts)]

            def load(j):
                return [src[j, p + 1] for p in range(parts)]

            def finish(j, tiles, moved):
                tiles = [tiles[0] + moved, *tiles[1:]]
                for p in range(parts):
                    cur[j, p] = tiles[p]
                if step + 1 < STEPS:
                    spread(dst, j, [t * inv_ref[step + 1, j, p] for p, t in enumerate(tiles)])

            near = [load(lo - 2 + b) for b in range(4)]
            bound = [scaled(near[1]), scaled(near[2])]
            term = south_terms(lo, near, bound)
            pending = []
            for j in range(lo, hi):
                near = [*near[1:], load(j + 2)]
                bound = [bound[1], scaled(near[2])]
                wide = [src[j, 0], *near[1], src[j, parts + 1], src[j, parts + 2]]
                limit = bound[0] + scaled([wide[parts + 1]])
                east = [east_ref[step, j, p] * face(*wide[p:p + 4], (limit[p], limit[p + 1]))
                        for p in range(parts)]
                moved = before(east[-1])
                following = south_terms(j + 1, near, bound)
                mass = entry(j) if step == 0 else [cur[j, p] for p in range(parts)]
                tiles = [mass[0] - (east[0] + (following[0] - term[0]))]
                tiles += [mass[p] - ((east[p] - east[p - 1]) + (following[p] - term[p])) for p in range(1, parts)]
                term = following
                pending.append((j, tiles, moved))
                if len(pending) > DELAY:
                    finish(*pending.pop(0))
            for one in pending:
                finish(*one)
            src, dst = dst, src
        for q in range(0, rows, 8):
            base = halo + q
            tiles = restore([cur[base:base + 8, p] for p in range(parts)])
            for p, tile in enumerate(tiles):
                out_ref[0, :, q:q + 8, p * LANES:(p + 1) * LANES] = jnp.swapaxes(tile, 0, 1)

    @pl.when(live & (flag > 0))
    def _():
        run(True)

    @pl.when(live & (flag <= 0))
    def _():
        run(False)

    @pl.when(jnp.logical_not(live))
    def _():
        out_ref[...] = jnp.zeros_like(out_ref)


def whole_block(shape):
    return pl.BlockSpec(shape, lambda *_: (0,) * len(shape))


def run_arrange(mass, first, count):
    _, levels, rows, columns = mass.shape
    batch = math.gcd(4, count, first)
    half = jax.ShapeDtypeStruct((count, rows // 2, columns // LANES, levels, LANES), jnp.float32)
    return pl.pallas_call(
        arrange_kernel,
        grid=(count // batch,),
        in_specs=[pl.BlockSpec((batch, levels, rows, columns), lambda i: (i + first // batch, 0, 0, 0))],
        out_specs=[pl.BlockSpec((batch, *half.shape[1:]), lambda i: (i, 0, 0, 0, 0))] * 2,
        out_shape=[half] * 2,
        name="arrange",
    )(mass)


def run_dynamics(place, own, north, south, level_block):
    planes, rows, columns = own.shape
    levels = planes // 3
    total = rows + 2 * HALO
    tiles = (total, columns // LANES, levels, LANES)
    flux = jax.ShapeDtypeStruct((STEPS, *tiles), jnp.float32)
    state = jax.ShapeDtypeStruct((level_block, rows, columns), jnp.float32)
    return pl.pallas_call(
        dynamics_kernel,
        grid_spec=pltpu.PrefetchScalarGridSpec(
            num_scalar_prefetch=1,
            grid=(1,),
            in_specs=[whole_block(own.shape), whole_block(north.shape), whole_block(south.shape)],
            out_specs=[pl.BlockSpec(memory_space=pltpu.VMEM)] * 3 + [whole_block(state.shape)] * 3,
            scratch_shapes=[pltpu.VMEM(tiles, jnp.float32)] * 7 + [pltpu.VMEM((3, levels, total, columns), jnp.float32)],
        ),
        out_shape=[flux] * 3 + [state] * 3,
        compiler_params=pltpu.CompilerParams(vmem_limit_bytes=48 << 20),
        name="dynamics",
    )(place, own, north, south)


def run_tracers(place, counts, flags, blocks, fluxes, first, out_shape, earlier):
    count, half, parts, levels, lanes = blocks[0].shape
    total = 2 * half + 2 * HALO
    in_specs = [pl.BlockSpec((1, *b.shape[1:]), lambda i, *_: (i, 0, 0, 0, 0)) for b in blocks]
    in_specs += [pl.BlockSpec(memory_space=pltpu.VMEM)] * len(fluxes)
    operands = [*blocks, *fluxes]
    aliases = {}
    if earlier is not None:
        aliases = {3 + len(operands): 0}
        in_specs.append(pl.BlockSpec(memory_space=pl.ANY))
        operands.append(earlier)
    wide = pltpu.VMEM((total, parts + 3, levels, lanes), jnp.float32)
    return pl.pallas_call(
        functools.partial(tracer_kernel, first=first),
        grid_spec=pltpu.PrefetchScalarGridSpec(
            num_scalar_prefetch=3,
            grid=(count,),
            in_specs=in_specs,
            out_specs=pl.BlockSpec((1, *out_shape[1:]), lambda i, *_: (i + first, 0, 0, 0)),
            scratch_shapes=[pltpu.VMEM((total, parts, levels, lanes), jnp.float32), wide, wide],
        ),
        out_shape=jax.ShapeDtypeStruct(out_shape, jnp.float32),
        input_output_aliases=aliases,
        compiler_params=pltpu.CompilerParams(vmem_limit_bytes=48 << 20),
        name="tracers",
    )(place, counts, flags, *operands)


def on_device(tracer_mass, layer_mass, zonal_wind, merid_wind, group_counts, limiter_flags):
    n_comp = lax.axis_size("comp")
    n_band = lax.axis_size("band")
    slots, levels, rows, _ = tracer_mass.shape
    level_block = layer_mass.shape[0]
    assert rows == 2 * HALO and levels == 8
    place = jnp.stack([
        lax.axis_index("comp"), lax.axis_index("band") * rows, jnp.int32(rows * n_band)
    ]).astype(jnp.int32)
    majors = n_comp // 2
    assert level_block == 1 and n_comp == levels and levels % 2 == 0

    def swap_minor(block):
        return lax.ppermute(block, "comp", [(i, i ^ 1) for i in range(n_comp)])

    def over_major(block):
        received = []
        for d in range(1, majors):
            received.append(lax.ppermute(block, "comp", [(i, (i + 2 * d) % n_comp) for i in range(n_comp)]))
        return lax.optimization_barrier(jnp.concatenate([block, *received], 0))

    chunk = slots // 2
    other_height = swap_minor(layer_mass)
    winds = over_major(jnp.concatenate([zonal_wind, merid_wind], 0))
    pair = lax.optimization_barrier(jnp.concatenate([layer_mass, other_height], 0))
    heights = over_major(pair)
    other_winds = swap_minor(winds)
    gathered = jnp.concatenate([winds, other_winds, heights], 0)
    from_north = band_shift(gathered[:, rows - HALO:], 1)
    from_south = band_shift(gathered[:, :HALO], -1)
    blocks = []
    for first in (0, chunk):
        top, bottom = run_arrange(tracer_mass, first, chunk)
        north = band_shift(bottom, 1)
        south = band_shift(top, -1)
        blocks.append((north, top, bottom, south))
    *fluxes, height, zonal, merid = run_dynamics(place, gathered, from_north, from_south, level_block)
    tracers = None
    for index, block in enumerate(blocks):
        tracers = run_tracers(place, group_counts, limiter_flags, block, fluxes, index * chunk,
                              tracer_mass.shape, tracers)
    return tracers, height, zonal, merid


def solution(mesh):
    placed = (
        P("comp", None, "band", None),
        P("comp", "band", None),
        P("comp", "band", None),
        P("comp", "band", None),
        P(),
        P(),
    )
    return jax.shard_map(
        on_device,
        mesh=mesh,
        in_specs=placed,
        out_specs=placed[:4],
        check_vma=False,
    )
```

```python
import functools
import math

import jax
import jax.numpy as jnp
from jax import lax
from jax.experimental import pallas as pl
from jax.experimental.pallas import tpu as pltpu
from jax.sharding import PartitionSpec as P


STEPS = 4
HALO = 2 * STEPS

time_step = 0.1
gravity = 0.25
coriolis = 0.5
mass_floor = 0.5


LANES = 128
DELAY = 3


def band_shift(block, offset):
    count = lax.axis_size("band")
    pairs = [(i, i + offset) for i in range(count) if 0 <= i + offset < count]
    return lax.ppermute(block, "band", pairs)


def lane_index(shape):
    return lax.broadcasted_iota(jnp.int32, shape, len(shape) - 1)


def swap_bits(tiles):
    tiles = list(tiles)
    lane = lane_index(tiles[0].shape)
    bit = 1
    while bit < len(tiles):
        keep = (lane & bit) == 0
        for a in range(len(tiles)):
            if not a & bit:
                b = a | bit
                first, second = tiles[a], tiles[b]
                axis = first.ndim - 1
                tiles[a] = jnp.where(keep, first, pltpu.roll(second, bit, axis))
                tiles[b] = jnp.where(keep, pltpu.roll(first, LANES - bit, axis), second)
        bit *= 2
    return tiles


def lane_order(shape, parts, inverse):
    lane = lane_index(shape)
    few, many = (parts, LANES // parts) if inverse else (LANES // parts, parts)
    return (lane & (few - 1)) * many + (lane >> (few.bit_length() - 1))


def take_lanes(tile, index):
    return jnp.take_along_axis(tile, index, axis=1, mode="promise_in_bounds")


def interleave(tiles):
    order = lane_order(tiles[0].shape[-2:], len(tiles), False)
    return [take_each(t, order) for t in swap_bits(tiles)]


def restore(tiles):
    order = lane_order(tiles[0].shape[-2:], len(tiles), True)
    return swap_bits([take_each(t, order) for t in tiles])


def take_each(tile, order):
    if tile.ndim == 2:
        return take_lanes(tile, order)
    return jnp.stack([take_lanes(tile[i], order) for i in range(tile.shape[0])])


def after(tile):
    return pltpu.roll(tile, LANES - 1, 1)


def before(tile):
    return pltpu.roll(tile, 1, 1)


def plane_order(levels):
    majors = levels // 2
    swapped = [(field, d, flip) for flip in range(2) for d in range(majors) for field in (1, 2)]
    return swapped + [(0, d, flip) for d in range(majors) for flip in range(2)]


def source_level(comp, levels, major, flip):
    majors = levels // 2
    at = (comp >> 1) - major
    return jnp.where(at < 0, at + majors, at) * 2 + ((comp & 1) ^ flip)


def split_row(row):
    return [row[..., p * LANES:(p + 1) * LANES] for p in range(row.shape[-1] // LANES)]


def arrange_kernel(mass, top, bottom):
    rows = mass.shape[2]
    half = rows // 2

    for t in range(mass.shape[0]):
        for out, base in ((top, 0), (bottom, half)):
            for q in range(0, half, 8):
                block = jnp.swapaxes(mass[t, :, base + q:base + q + 8], 0, 1)
                for p, tile in enumerate(interleave(split_row(block))):
                    out[t, q:q + 8, p] = tile


def run_dynamics(place, own, north, south, h_out, u_out, v_out, inv_ref, east_ref, south_ref,
                 h0, u0, v0, h1, u1, v1, geo, stage):
    planes, rows, columns = own.shape
    parts = columns // LANES
    halo = north.shape[1]
    total = rows + 2 * halo
    levels = planes // 3
    for plane, (field, major, flip) in enumerate(plane_order(levels)):
        level = source_level(place[0], levels, major, flip)
        for source, base in ((north, 0), (own, halo), (south, halo + rows)):
            stage[field, level, base:base + source.shape[1]] = source[plane]
    for field, dst in enumerate((h0, u0, v0)):
        for q in range(0, total, 8):
            block = jnp.swapaxes(stage[field, :, q:q + 8], 0, 1)
            for p, tile in enumerate(interleave(split_row(block))):
                dst[q:q + 8, p] = tile
    first_face = place[1] - halo
    scales = [jnp.where((first_face + j > 0) & (first_face + j < place[2]), 0.25 * time_step, 0.0)
              for j in range(total)]
    level = lax.broadcasted_iota(jnp.int32, (levels, LANES), 0)
    src, dst = (h0, u0, v0), (h1, u1, v1)
    for step in range(STEPS):
        h, u, v = src
        lo, hi = 2 * (step + 1), total - 2 * (step + 1)

        def column(j):
            for p in range(parts):
                hp = h[j, p]
                acc = hp
                span = 1
                while span < levels:
                    moved = pltpu.roll(acc, levels - span, 0)
                    acc = acc + jnp.where(level < levels - span, moved, 0.0)
                    span *= 2
                geo[j, p] = gravity * acc
                inv_ref[step, j, p] = (1.0 / 12.0) / jnp.maximum(hp, mass_floor)

        def south_flux(j):
            return [scales[j] * (v[j - 1, p] + v[j, p]) * (h[j - 1, p] + h[j, p]) for p in range(parts)]

        def finish(j, tiles, moved):
            dst[0][j, 0] = tiles[0] + moved
            for p in range(1, parts):
                dst[0][j, p] = tiles[p]

        for j in range(lo - 2, lo + 1):
            column(j)
        flux_north = south_flux(lo)
        pending = []
        for j in range(lo, hi):
            column(j + 1)
            hj, uj, vj, gj = ([f[j, p] for p in range(parts)] for f in (h, u, v, geo))
            hj.append(after(hj[0]))
            uj.append(after(uj[0]))
            gj = [before(gj[-1]), *gj, after(gj[0])]
            flux = south_flux(j + 1)
            east = [(0.25 * time_step) * (uj[p] + uj[p + 1]) * (hj[p] + hj[p + 1]) for p in range(parts)]
            tiles = [hj[0] - (east[0] + (flux[0] - flux_north[0]))]
            tiles += [hj[p] - ((east[p] - east[p - 1]) + (flux[p] - flux_north[p])) for p in range(1, parts)]
            pending.append((j, tiles, before(east[-1])))
            for p in range(parts):
                east_ref[step, j, p] = east[p]
                south_ref[step, j, p] = flux_north[p]
                slope_x = gj[p + 2] - gj[p]
                slope_y = geo[j + 1, p] - geo[j - 1, p]
                dst[1][j, p] = uj[p] + time_step * (coriolis * vj[p] - 0.5 * slope_x)
                dst[2][j, p] = vj[p] - time_step * (coriolis * uj[p] + 0.5 * slope_y)
            flux_north = flux
            if len(pending) > DELAY:
                finish(*pending.pop(0))
        for one in pending:
            finish(*one)
        for p in range(parts):
            south_ref[step, hi, p] = flux_north[p]
        column(hi + 1)
        src, dst = dst, src
    block = h_out.shape[0]
    for out, field in zip((h_out, u_out, v_out), src):
        for k in range(block):
            mine = pl.ds(place[0] * block + k, 1)
            for q in range(0, rows, 8):
                tiles = restore([
                    jnp.concatenate([field[halo + q + i, p, mine, :] for i in range(8)], 0) for p in range(parts)])
                for p, tile in enumerate(tiles):
                    out[k, q:q + 8, p * LANES:(p + 1) * LANES] = tile


def tracer_kernel(place, counts, flags, *refs, first, lead):
    step_id = pl.program_id(0)
    if lead:
        planes, (north, top, bottom, south, out_ref), refs = refs[:3], refs[3:8], refs[8:]
        states, kept, refs = refs[:3], refs[3:6], refs[6:]
    else:
        kept, (north, top, bottom, south, _, out_ref), refs = refs[:3], refs[3:9], refs[9:]
    (cur, even, odd), fluxes, done, work = refs[:3], refs[3:6], refs[6], refs[7:]
    pairs = zip(fluxes, kept) if lead else zip(kept, fluxes)
    copies = [pltpu.make_async_copy(a, b, done.at[i]) for i, (a, b) in enumerate(pairs)]

    @pl.when(step_id == 0)
    def _():
        if lead:
            run_dynamics(place, *planes, *states, *fluxes, *work)
        for copy in copies:
            copy.start()
        if not lead:
            for copy in copies:
                copy.wait()

    inv_ref, east_ref, south_ref = fluxes
    slot = step_id + first
    parts = north.shape[2]
    halo = north.shape[1]
    half = top.shape[1]
    rows = 2 * half
    total = rows + 2 * halo
    group = place[0]
    start = jnp.int32(0)
    for g in range(counts.shape[0]):
        start = start + jnp.where(g < group, counts[g], 0)
    live = slot < counts[group]
    flag = flags[jnp.minimum(start + slot, flags.shape[0] - 1)]

    def entry(j):
        for source, base in ((south, halo + rows), (bottom, halo + half), (top, halo), (north, 0)):
            if j >= base:
                return [source[0, j - base, p] for p in range(parts)]

    def run(limited):
        def spread(buffer, j, tiles):
            for p in range(parts):
                buffer[j, p + 1] = tiles[p]
            buffer[j, 0] = before(tiles[-1])
            buffer[j, parts + 1] = after(tiles[0])
            buffer[j, parts + 2] = after(tiles[1])

        for j in range(total):
            spread(even, j, [t * inv_ref[0, j, p] for p, t in enumerate(entry(j))])

        def face(a2, a, b, b2, bounds):
            raw = 7.0 * (a + b) - (a2 + b2)
            if limited:
                raw = jnp.minimum(jnp.maximum(raw, jnp.minimum(*bounds)), jnp.maximum(*bounds))
            return raw

        def scaled(tiles):
            return [12.0 * t for t in tiles] if limited else [None] * len(tiles)

        src, dst = even, odd
        for step in range(STEPS):
            lo, hi = 2 * (step + 1), total - 2 * (step + 1)

            def south_terms(j, near, bounds):
                return [south_ref[step, j, p] * face(*(t[p] for t in near), tuple(t[p] for t in bounds))
                        for p in range(parts)]

            def load(j):
                return [src[j, p + 1] for p in range(parts)]

            def finish(j, tiles, moved):
                tiles = [tiles[0] + moved, *tiles[1:]]
                for p in range(parts):
                    cur[j, p] = tiles[p]
                if step + 1 < STEPS:
                    spread(dst, j, [t * inv_ref[step + 1, j, p] for p, t in enumerate(tiles)])

            near = [load(lo - 2 + b) for b in range(4)]
            bound = [scaled(near[1]), scaled(near[2])]
            term = south_terms(lo, near, bound)
            pending = []
            for j in range(lo, hi):
                near = [*near[1:], load(j + 2)]
                bound = [bound[1], scaled(near[2])]
                wide = [src[j, 0], *near[1], src[j, parts + 1], src[j, parts + 2]]
                limit = bound[0] + scaled([wide[parts + 1]])
                east = [east_ref[step, j, p] * face(*wide[p:p + 4], (limit[p], limit[p + 1]))
                        for p in range(parts)]
                moved = before(east[-1])
                following = south_terms(j + 1, near, bound)
                mass = entry(j) if step == 0 else [cur[j, p] for p in range(parts)]
                tiles = [mass[0] - (east[0] + (following[0] - term[0]))]
                tiles += [mass[p] - ((east[p] - east[p - 1]) + (following[p] - term[p])) for p in range(1, parts)]
                term = following
                pending.append((j, tiles, moved))
                if len(pending) > DELAY:
                    finish(*pending.pop(0))
            for one in pending:
                finish(*one)
            src, dst = dst, src
        for q in range(0, rows, 8):
            base = halo + q
            tiles = restore([cur[base:base + 8, p] for p in range(parts)])
            for p, tile in enumerate(tiles):
                out_ref[0, :, q:q + 8, p * LANES:(p + 1) * LANES] = jnp.swapaxes(tile, 0, 1)

    @pl.when(live & (flag > 0))
    def _():
        run(True)

    @pl.when(live & (flag <= 0))
    def _():
        run(False)

    @pl.when(jnp.logical_not(live))
    def _():
        out_ref[...] = jnp.zeros_like(out_ref)

    if lead:
        @pl.when(step_id == pl.num_programs(0) - 1)
        def _():
            for copy in copies:
                copy.wait()


def whole_block(shape):
    return pl.BlockSpec(shape, lambda *_: (0,) * len(shape))


def run_arrange(mass, first, count):
    _, levels, rows, columns = mass.shape
    batch = math.gcd(4, count, first)
    half = jax.ShapeDtypeStruct((count, rows // 2, columns // LANES, levels, LANES), jnp.float32)
    return pl.pallas_call(
        arrange_kernel,
        grid=(count // batch,),
        in_specs=[pl.BlockSpec((batch, levels, rows, columns), lambda i: (i + first // batch, 0, 0, 0))],
        out_specs=[pl.BlockSpec((batch, *half.shape[1:]), lambda i: (i, 0, 0, 0, 0))] * 2,
        out_shape=[half] * 2,
        name="arrange",
    )(mass)


def run_tracers(place, counts, flags, blocks, planes, kept, earlier, first, out_shape):
    lead = planes is not None
    count, half, parts, levels, lanes = blocks[0].shape
    rows, columns = 2 * half, parts * lanes
    total = rows + 2 * HALO
    tiles = (total, parts, levels, lanes)
    wide = (total, parts + 3, levels, lanes)
    anywhere = pl.BlockSpec(memory_space=pl.ANY)
    block_specs = [pl.BlockSpec((1, *b.shape[1:]), lambda i, *_: (i, 0, 0, 0, 0)) for b in blocks]
    out_specs = [pl.BlockSpec((1, *out_shape[1:]), lambda i, *_: (i + first, 0, 0, 0))]
    out_types = [jax.ShapeDtypeStruct(out_shape, jnp.float32)]
    scratch = [tiles, wide, wide] + [(STEPS, *tiles)] * 3
    scratch = [pltpu.VMEM(s, jnp.float32) for s in scratch] + [pltpu.SemaphoreType.DMA((3,))]
    aliases = {}
    if lead:
        state = (1, rows, columns)
        operands = [*planes, *blocks]
        in_specs = [whole_block(p.shape) for p in planes] + block_specs
        out_specs += [whole_block(state)] * 3 + [anywhere] * 3
        out_types += [jax.ShapeDtypeStruct(state, jnp.float32)] * 3
        out_types += [jax.ShapeDtypeStruct((STEPS, *tiles), jnp.float32)] * 3
        work = [tiles] * 7 + [(3, levels, total, columns)]
        scratch += [pltpu.VMEM(s, jnp.float32) for s in work]
    else:
        operands = [*kept, *blocks, earlier]
        in_specs = [anywhere] * 3 + block_specs + [anywhere]
        aliases = {2 + len(operands): 0}
    return pl.pallas_call(
        functools.partial(tracer_kernel, first=first, lead=lead),
        grid_spec=pltpu.PrefetchScalarGridSpec(
            num_scalar_prefetch=3,
            grid=(count,),
            in_specs=in_specs,
            out_specs=out_specs,
            scratch_shapes=scratch,
        ),
        out_shape=out_types,
        input_output_aliases=aliases,
        compiler_params=pltpu.CompilerParams(vmem_limit_bytes=52 << 20),
        name="tracers",
    )(place, counts, flags, *operands)


def on_device(tracer_mass, layer_mass, zonal_wind, merid_wind, group_counts, limiter_flags):
    n_comp = lax.axis_size("comp")
    n_band = lax.axis_size("band")
    slots, levels, rows, _ = tracer_mass.shape
    level_block = layer_mass.shape[0]
    assert rows == 2 * HALO and levels == 8
    place = jnp.stack([
        lax.axis_index("comp"), lax.axis_index("band") * rows, jnp.int32(rows * n_band)
    ]).astype(jnp.int32)
    majors = n_comp // 2
    assert level_block == 1 and n_comp == levels and levels % 2 == 0

    def swap_minor(block):
        return lax.ppermute(block, "comp", [(i, i ^ 1) for i in range(n_comp)])

    def over_major(block):
        received = []
        for d in range(1, majors):
            received.append(lax.ppermute(block, "comp", [(i, (i + 2 * d) % n_comp) for i in range(n_comp)]))
        return lax.optimization_barrier(jnp.concatenate([block, *received], 0))

    chunk = slots // 2
    other_height = swap_minor(layer_mass)
    winds = over_major(jnp.concatenate([zonal_wind, merid_wind], 0))
    pair = lax.optimization_barrier(jnp.concatenate([layer_mass, other_height], 0))
    heights = over_major(pair)
    other_winds = swap_minor(winds)
    gathered = jnp.concatenate([winds, other_winds, heights], 0)
    from_north = band_shift(gathered[:, rows - HALO:], 1)
    from_south = band_shift(gathered[:, :HALO], -1)
    blocks = []
    for first in (0, chunk):
        top, bottom = run_arrange(tracer_mass, first, chunk)
        north = band_shift(bottom, 1)
        south = band_shift(top, -1)
        blocks.append((north, top, bottom, south))
    planes = (gathered, from_north, from_south)
    earlier, height, zonal, merid, *kept = run_tracers(
        place, group_counts, limiter_flags, blocks[0], planes, None, None, 0, tracer_mass.shape)
    tracers, = run_tracers(
        place, group_counts, limiter_flags, blocks[1], None, kept, earlier, chunk, tracer_mass.shape)
    return tracers, height, zonal, merid


def solution(mesh):
    placed = (
        P("comp", None, "band", None),
        P("comp", "band", None),
        P("comp", "band", None),
        P("comp", "band", None),
        P(),
        P(),
    )
    return jax.shard_map(
        on_device,
        mesh=mesh,
        in_specs=placed,
        out_specs=placed[:4],
        check_vma=False,
    )
```

```python
import functools
import math

import jax
import jax.numpy as jnp
from jax import lax
from jax.experimental import pallas as pl
from jax.experimental.pallas import tpu as pltpu
from jax.sharding import PartitionSpec as P


STEPS = 4
HALO = 2 * STEPS

time_step = 0.1
gravity = 0.25
coriolis = 0.5
mass_floor = 0.5


LANES = 128
DELAY = 3


def band_shift(block, offset):
    count = lax.axis_size("band")
    pairs = [(i, i + offset) for i in range(count) if 0 <= i + offset < count]
    return lax.ppermute(block, "band", pairs)


def lane_index(shape):
    return lax.broadcasted_iota(jnp.int32, shape, len(shape) - 1)


def swap_bits(tiles):
    tiles = list(tiles)
    lane = lane_index(tiles[0].shape)
    bit = 1
    while bit < len(tiles):
        keep = (lane & bit) == 0
        for a in range(len(tiles)):
            if not a & bit:
                b = a | bit
                first, second = tiles[a], tiles[b]
                axis = first.ndim - 1
                tiles[a] = jnp.where(keep, first, pltpu.roll(second, bit, axis))
                tiles[b] = jnp.where(keep, pltpu.roll(first, LANES - bit, axis), second)
        bit *= 2
    return tiles


def lane_order(shape, parts, inverse):
    lane = lane_index(shape)
    few, many = (parts, LANES // parts) if inverse else (LANES // parts, parts)
    return (lane & (few - 1)) * many + (lane >> (few.bit_length() - 1))


def take_lanes(tile, index):
    return jnp.take_along_axis(tile, index, axis=1, mode="promise_in_bounds")


def interleave(tiles):
    order = lane_order(tiles[0].shape[-2:], len(tiles), False)
    return [take_each(t, order) for t in swap_bits(tiles)]


def restore(tiles):
    order = lane_order(tiles[0].shape[-2:], len(tiles), True)
    return swap_bits([take_each(t, order) for t in tiles])


def take_each(tile, order):
    if tile.ndim == 2:
        return take_lanes(tile, order)
    return jnp.stack([take_lanes(tile[i], order) for i in range(tile.shape[0])])


def after(tile):
    return pltpu.roll(tile, LANES - 1, 1)


def before(tile):
    return pltpu.roll(tile, 1, 1)


def plane_order(levels):
    return [(field, d, flip) for flip in range(2) for d in range(levels // 2) for field in range(3)]


def source_level(comp, levels, major, flip):
    majors = levels // 2
    at = (comp >> 1) - major
    return jnp.where(at < 0, at + majors, at) * 2 + ((comp & 1) ^ flip)


def split_row(row):
    return [row[..., p * LANES:(p + 1) * LANES] for p in range(row.shape[-1] // LANES)]


def arrange_kernel(mass, top, bottom):
    rows = mass.shape[2]
    half = rows // 2

    for t in range(mass.shape[0]):
        for out, base in ((top, 0), (bottom, half)):
            for q in range(0, half, 8):
                block = jnp.swapaxes(mass[t, :, base + q:base + q + 8], 0, 1)
                for p, tile in enumerate(interleave(split_row(block))):
                    out[t, q:q + 8, p] = tile


def run_dynamics(place, own, north, south, h_out, u_out, v_out, inv_ref, east_ref, south_ref,
                 h0, u0, v0, h1, u1, v1, geo, stage):
    planes, rows, columns = own.shape
    parts = columns // LANES
    halo = north.shape[1]
    total = rows + 2 * halo
    levels = planes // 3
    for plane, (field, major, flip) in enumerate(plane_order(levels)):
        level = source_level(place[0], levels, major, flip)
        for source, base in ((north, 0), (own, halo), (south, halo + rows)):
            stage[field, level, base:base + source.shape[1]] = source[plane]
    for field, dst in enumerate((h0, u0, v0)):
        for q in range(0, total, 8):
            block = jnp.swapaxes(stage[field, :, q:q + 8], 0, 1)
            for p, tile in enumerate(interleave(split_row(block))):
                dst[q:q + 8, p] = tile
    first_face = place[1] - halo
    scales = [jnp.where((first_face + j > 0) & (first_face + j < place[2]), 0.25 * time_step, 0.0)
              for j in range(total)]
    level = lax.broadcasted_iota(jnp.int32, (levels, LANES), 0)
    src, dst = (h0, u0, v0), (h1, u1, v1)
    for step in range(STEPS):
        h, u, v = src
        lo, hi = 2 * (step + 1), total - 2 * (step + 1)

        def column(j):
            for p in range(parts):
                hp = h[j, p]
                acc = hp
                span = 1
                while span < levels:
                    moved = pltpu.roll(acc, levels - span, 0)
                    acc = acc + jnp.where(level < levels - span, moved, 0.0)
                    span *= 2
                geo[j, p] = gravity * acc
                inv_ref[step, j, p] = (1.0 / 12.0) / jnp.maximum(hp, mass_floor)

        def south_flux(j):
            return [scales[j] * (v[j - 1, p] + v[j, p]) * (h[j - 1, p] + h[j, p]) for p in range(parts)]

        def finish(j, tiles, moved):
            dst[0][j, 0] = tiles[0] + moved
            for p in range(1, parts):
                dst[0][j, p] = tiles[p]

        for j in range(lo - 2, lo + 1):
            column(j)
        flux_north = south_flux(lo)
        pending = []
        for j in range(lo, hi):
            column(j + 1)
            hj, uj, vj, gj = ([f[j, p] for p in range(parts)] for f in (h, u, v, geo))
            hj.append(after(hj[0]))
            uj.append(after(uj[0]))
            gj = [before(gj[-1]), *gj, after(gj[0])]
            flux = south_flux(j + 1)
            east = [(0.25 * time_step) * (uj[p] + uj[p + 1]) * (hj[p] + hj[p + 1]) for p in range(parts)]
            tiles = [hj[0] - (east[0] + (flux[0] - flux_north[0]))]
            tiles += [hj[p] - ((east[p] - east[p - 1]) + (flux[p] - flux_north[p])) for p in range(1, parts)]
            pending.append((j, tiles, before(east[-1])))
            for p in range(parts):
                east_ref[step, j, p] = east[p]
                south_ref[step, j, p] = flux_north[p]
                slope_x = gj[p + 2] - gj[p]
                slope_y = geo[j + 1, p] - geo[j - 1, p]
                dst[1][j, p] = uj[p] + time_step * (coriolis * vj[p] - 0.5 * slope_x)
                dst[2][j, p] = vj[p] - time_step * (coriolis * uj[p] + 0.5 * slope_y)
            flux_north = flux
            if len(pending) > DELAY:
                finish(*pending.pop(0))
        for one in pending:
            finish(*one)
        for p in range(parts):
            south_ref[step, hi, p] = flux_north[p]
        column(hi + 1)
        src, dst = dst, src
    block = h_out.shape[0]
    for out, field in zip((h_out, u_out, v_out), src):
        for k in range(block):
            mine = pl.ds(place[0] * block + k, 1)
            for q in range(0, rows, 8):
                tiles = restore([
                    jnp.concatenate([field[halo + q + i, p, mine, :] for i in range(8)], 0) for p in range(parts)])
                for p, tile in enumerate(tiles):
                    out[k, q:q + 8, p * LANES:(p + 1) * LANES] = tile


def tracer_kernel(place, counts, flags, *refs, first, lead):
    step_id = pl.program_id(0)
    if lead:
        planes, (north, top, bottom, south, out_ref), refs = refs[:3], refs[3:8], refs[8:]
        states, kept, refs = refs[:3], refs[3:6], refs[6:]
    else:
        kept, (north, top, bottom, south, _, out_ref), refs = refs[:3], refs[3:9], refs[9:]
    (cur, even, odd), fluxes, done, work = refs[:3], refs[3:6], refs[6], refs[7:]
    pairs = zip(fluxes, kept) if lead else zip(kept, fluxes)
    copies = [pltpu.make_async_copy(a, b, done.at[i]) for i, (a, b) in enumerate(pairs)]

    @pl.when(step_id == 0)
    def _():
        if lead:
            run_dynamics(place, *planes, *states, *fluxes, *work)
        for copy in copies:
            copy.start()
        if not lead:
            for copy in copies:
                copy.wait()

    inv_ref, east_ref, south_ref = fluxes
    slot = step_id + first
    parts = north.shape[2]
    halo = north.shape[1]
    half = top.shape[1]
    rows = 2 * half
    total = rows + 2 * halo
    group = place[0]
    start = jnp.int32(0)
    for g in range(counts.shape[0]):
        start = start + jnp.where(g < group, counts[g], 0)
    live = slot < counts[group]
    flag = flags[jnp.minimum(start + slot, flags.shape[0] - 1)]

    def entry(j):
        for source, base in ((south, halo + rows), (bottom, halo + half), (top, halo), (north, 0)):
            if j >= base:
                return [source[0, j - base, p] for p in range(parts)]

    def run(limited):
        def spread(buffer, j, tiles):
            for p in range(parts):
                buffer[j, p + 1] = tiles[p]
            buffer[j, 0] = before(tiles[-1])
            buffer[j, parts + 1] = after(tiles[0])
            buffer[j, parts + 2] = after(tiles[1])

        for j in range(total):
            spread(even, j, [t * inv_ref[0, j, p] for p, t in enumerate(entry(j))])

        def face(a2, a, b, b2, bounds):
            raw = 7.0 * (a + b) - (a2 + b2)
            if limited:
                raw = jnp.minimum(jnp.maximum(raw, jnp.minimum(*bounds)), jnp.maximum(*bounds))
            return raw

        def scaled(tiles):
            return [12.0 * t for t in tiles] if limited else [None] * len(tiles)

        src, dst = even, odd
        for step in range(STEPS):
            lo, hi = 2 * (step + 1), total - 2 * (step + 1)

            def south_terms(j, near, bounds):
                return [south_ref[step, j, p] * face(*(t[p] for t in near), tuple(t[p] for t in bounds))
                        for p in range(parts)]

            def load(j):
                return [src[j, p + 1] for p in range(parts)]

            def finish(j, tiles, moved):
                tiles = [tiles[0] + moved, *tiles[1:]]
                for p in range(parts):
                    cur[j, p] = tiles[p]
                if step + 1 < STEPS:
                    spread(dst, j, [t * inv_ref[step + 1, j, p] for p, t in enumerate(tiles)])

            near = [load(lo - 2 + b) for b in range(4)]
            bound = [scaled(near[1]), scaled(near[2])]
            term = south_terms(lo, near, bound)
            pending = []
            for j in range(lo, hi):
                near = [*near[1:], load(j + 2)]
                bound = [bound[1], scaled(near[2])]
                wide = [src[j, 0], *near[1], src[j, parts + 1], src[j, parts + 2]]
                limit = bound[0] + scaled([wide[parts + 1]])
                east = [east_ref[step, j, p] * face(*wide[p:p + 4], (limit[p], limit[p + 1]))
                        for p in range(parts)]
                moved = before(east[-1])
                following = south_terms(j + 1, near, bound)
                mass = entry(j) if step == 0 else [cur[j, p] for p in range(parts)]
                tiles = [mass[0] - (east[0] + (following[0] - term[0]))]
                tiles += [mass[p] - ((east[p] - east[p - 1]) + (following[p] - term[p])) for p in range(1, parts)]
                term = following
                pending.append((j, tiles, moved))
                if len(pending) > DELAY:
                    finish(*pending.pop(0))
            for one in pending:
                finish(*one)
            src, dst = dst, src
        for q in range(0, rows, 8):
            base = halo + q
            tiles = restore([cur[base:base + 8, p] for p in range(parts)])
            for p, tile in enumerate(tiles):
                out_ref[0, :, q:q + 8, p * LANES:(p + 1) * LANES] = jnp.swapaxes(tile, 0, 1)

    @pl.when(live & (flag > 0))
    def _():
        run(True)

    @pl.when(live & (flag <= 0))
    def _():
        run(False)

    @pl.when(jnp.logical_not(live))
    def _():
        out_ref[...] = jnp.zeros_like(out_ref)

    if lead:
        @pl.when(step_id == pl.num_programs(0) - 1)
        def _():
            for copy in copies:
                copy.wait()


def whole_block(shape):
    return pl.BlockSpec(shape, lambda *_: (0,) * len(shape))


def run_arrange(mass, first, count):
    _, levels, rows, columns = mass.shape
    batch = math.gcd(4, count, first)
    half = jax.ShapeDtypeStruct((count, rows // 2, columns // LANES, levels, LANES), jnp.float32)
    return pl.pallas_call(
        arrange_kernel,
        grid=(count // batch,),
        in_specs=[pl.BlockSpec((batch, levels, rows, columns), lambda i: (i + first // batch, 0, 0, 0))],
        out_specs=[pl.BlockSpec((batch, *half.shape[1:]), lambda i: (i, 0, 0, 0, 0))] * 2,
        out_shape=[half] * 2,
        name="arrange",
    )(mass)


def run_tracers(place, counts, flags, blocks, planes, kept, earlier, first, out_shape):
    lead = planes is not None
    count, half, parts, levels, lanes = blocks[0].shape
    rows, columns = 2 * half, parts * lanes
    total = rows + 2 * HALO
    tiles = (total, parts, levels, lanes)
    wide = (total, parts + 3, levels, lanes)
    anywhere = pl.BlockSpec(memory_space=pl.ANY)
    block_specs = [pl.BlockSpec((1, *b.shape[1:]), lambda i, *_: (i, 0, 0, 0, 0)) for b in blocks]
    out_specs = [pl.BlockSpec((1, *out_shape[1:]), lambda i, *_: (i + first, 0, 0, 0))]
    out_types = [jax.ShapeDtypeStruct(out_shape, jnp.float32)]
    scratch = [tiles, wide, wide] + [(STEPS, *tiles)] * 3
    scratch = [pltpu.VMEM(s, jnp.float32) for s in scratch] + [pltpu.SemaphoreType.DMA((3,))]
    aliases = {}
    if lead:
        state = (1, rows, columns)
        operands = [*planes, *blocks]
        in_specs = [whole_block(p.shape) for p in planes] + block_specs
        out_specs += [whole_block(state)] * 3 + [anywhere] * 3
        out_types += [jax.ShapeDtypeStruct(state, jnp.float32)] * 3
        out_types += [jax.ShapeDtypeStruct((STEPS, *tiles), jnp.float32)] * 3
        work = [tiles] * 7 + [(3, levels, total, columns)]
        scratch += [pltpu.VMEM(s, jnp.float32) for s in work]
    else:
        operands = [*kept, *blocks, earlier]
        in_specs = [anywhere] * 3 + block_specs + [anywhere]
        aliases = {2 + len(operands): 0}
    return pl.pallas_call(
        functools.partial(tracer_kernel, first=first, lead=lead),
        grid_spec=pltpu.PrefetchScalarGridSpec(
            num_scalar_prefetch=3,
            grid=(count,),
            in_specs=in_specs,
            out_specs=out_specs,
            scratch_shapes=scratch,
        ),
        out_shape=out_types,
        input_output_aliases=aliases,
        compiler_params=pltpu.CompilerParams(vmem_limit_bytes=52 << 20),
        name="tracers",
    )(place, counts, flags, *operands)


def on_device(tracer_mass, layer_mass, zonal_wind, merid_wind, group_counts, limiter_flags):
    n_comp = lax.axis_size("comp")
    n_band = lax.axis_size("band")
    slots, levels, rows, _ = tracer_mass.shape
    level_block = layer_mass.shape[0]
    assert rows == 2 * HALO and levels == 8
    place = jnp.stack([
        lax.axis_index("comp"), lax.axis_index("band") * rows, jnp.int32(rows * n_band)
    ]).astype(jnp.int32)
    majors = n_comp // 2
    assert level_block == 1 and n_comp == levels and levels % 2 == 0

    def swap_minor(block):
        return lax.ppermute(block, "comp", [(i, i ^ 1) for i in range(n_comp)])

    def over_major(block):
        received = []
        for d in range(1, majors):
            received.append(lax.ppermute(block, "comp", [(i, (i + 2 * d) % n_comp) for i in range(n_comp)]))
        return lax.optimization_barrier(jnp.concatenate([block, *received], 0))

    chunk = slots // 3
    near = over_major(jnp.concatenate([layer_mass, zonal_wind, merid_wind], 0))
    far = swap_minor(near)
    gathered = jnp.concatenate([near, far], 0)
    from_north = band_shift(gathered[:, rows - HALO:], 1)
    from_south = band_shift(gathered[:, :HALO], -1)
    blocks = []
    for first, count in ((0, chunk), (chunk, slots - chunk)):
        top, bottom = run_arrange(tracer_mass, first, count)
        north = band_shift(bottom, 1)
        south = band_shift(top, -1)
        blocks.append((north, top, bottom, south))
    planes = (gathered, from_north, from_south)
    earlier, height, zonal, merid, *kept = run_tracers(
        place, group_counts, limiter_flags, blocks[0], planes, None, None, 0, tracer_mass.shape)
    tracers, = run_tracers(
        place, group_counts, limiter_flags, blocks[1], None, kept, earlier, chunk, tracer_mass.shape)
    return tracers, height, zonal, merid


def solution(mesh):
    placed = (
        P("comp", None, "band", None),
        P("comp", "band", None),
        P("comp", "band", None),
        P("comp", "band", None),
        P(),
        P(),
    )
    return jax.shard_map(
        on_device,
        mesh=mesh,
        in_specs=placed,
        out_specs=placed[:4],
        check_vma=False,
    )
```

```python
import functools
import math

import jax
import jax.numpy as jnp
from jax import lax
from jax.experimental import pallas as pl
from jax.experimental.pallas import tpu as pltpu
from jax.sharding import PartitionSpec as P


STEPS = 4
HALO = 2 * STEPS

time_step = 0.1
gravity = 0.25
coriolis = 0.5
mass_floor = 0.5


LANES = 128
DELAY = 6
BATCH = 1


def band_shift(block, offset):
    count = lax.axis_size("band")
    pairs = [(i, i + offset) for i in range(count) if 0 <= i + offset < count]
    return lax.ppermute(block, "band", pairs)


def lane_index(shape):
    return lax.broadcasted_iota(jnp.int32, shape, len(shape) - 1)


def swap_bits(tiles):
    tiles = list(tiles)
    lane = lane_index(tiles[0].shape)
    bit = 1
    while bit < len(tiles):
        keep = (lane & bit) == 0
        for a in range(len(tiles)):
            if not a & bit:
                b = a | bit
                first, second = tiles[a], tiles[b]
                axis = first.ndim - 1
                tiles[a] = jnp.where(keep, first, pltpu.roll(second, bit, axis))
                tiles[b] = jnp.where(keep, pltpu.roll(first, LANES - bit, axis), second)
        bit *= 2
    return tiles


def lane_order(shape, parts, inverse):
    lane = lane_index(shape)
    few, many = (parts, LANES // parts) if inverse else (LANES // parts, parts)
    return (lane & (few - 1)) * many + (lane >> (few.bit_length() - 1))


def take_lanes(tile, index):
    return jnp.take_along_axis(tile, index, axis=1, mode="promise_in_bounds")


def interleave(tiles):
    order = lane_order(tiles[0].shape[-2:], len(tiles), False)
    return [take_each(t, order) for t in swap_bits(tiles)]


def restore(tiles):
    order = lane_order(tiles[0].shape[-2:], len(tiles), True)
    return swap_bits([take_each(t, order) for t in tiles])


def take_each(tile, order):
    if tile.ndim == 2:
        return take_lanes(tile, order)
    return jnp.stack([take_lanes(tile[i], order) for i in range(tile.shape[0])])


def after(tile):
    return pltpu.roll(tile, LANES - 1, 1)


def before(tile):
    return pltpu.roll(tile, 1, 1)


def plane_order(levels):
    return [(field, d, flip) for flip in range(2) for d in range(levels // 2) for field in range(3)]


def source_level(comp, levels, major, flip):
    majors = levels // 2
    at = (comp >> 1) - major
    return jnp.where(at < 0, at + majors, at) * 2 + ((comp & 1) ^ flip)


def split_row(row):
    return [row[..., p * LANES:(p + 1) * LANES] for p in range(row.shape[-1] // LANES)]


def arrange_kernel(mass, top, bottom):
    rows = mass.shape[2]
    half = rows // 2

    for t in range(mass.shape[0]):
        for out, base in ((top, 0), (bottom, half)):
            for q in range(0, half, 8):
                block = jnp.swapaxes(mass[t, :, base + q:base + q + 8], 0, 1)
                for p, tile in enumerate(interleave(split_row(block))):
                    out[t, q:q + 8, p] = tile


def run_dynamics(place, state, near, far_state, far, north, south, h_out, u_out, v_out, inv_ref, east_ref, south_ref,
                 h0, u0, v0, h1, u1, v1, geo, stage):
    planes, rows, columns = north.shape[0], *near.shape[1:]
    parts = columns // LANES
    halo = north.shape[1]
    total = rows + 2 * halo
    levels = planes // 3
    sources = [(piece, i) for piece in (state, near, far_state, far) for i in range(piece.shape[0])]
    for plane, (field, major, flip) in enumerate(plane_order(levels)):
        level = source_level(place[0], levels, major, flip)
        own = sources[plane][0][sources[plane][1]]
        for block, base in ((north[plane], 0), (own, halo), (south[plane], halo + rows)):
            stage[field, level, base:base + block.shape[0]] = block
    for field, dst in enumerate((h0, u0, v0)):
        for q in range(0, total, 8):
            block = jnp.swapaxes(stage[field, :, q:q + 8], 0, 1)
            for p, tile in enumerate(interleave(split_row(block))):
                dst[q:q + 8, p] = tile
    first_face = place[1] - halo
    scales = [jnp.where((first_face + j > 0) & (first_face + j < place[2]), 0.25 * time_step, 0.0)
              for j in range(total)]
    level = lax.broadcasted_iota(jnp.int32, (levels, LANES), 0)
    src, dst = (h0, u0, v0), (h1, u1, v1)
    for step in range(STEPS):
        h, u, v = src
        lo, hi = 2 * (step + 1), total - 2 * (step + 1)

        def column(j):
            for p in range(parts):
                hp = h[j, p]
                acc = hp
                span = 1
                while span < levels:
                    moved = pltpu.roll(acc, levels - span, 0)
                    acc = acc + jnp.where(level < levels - span, moved, 0.0)
                    span *= 2
                geo[j, p] = gravity * acc
                inv_ref[step, j, p] = (1.0 / 12.0) / jnp.maximum(hp, mass_floor)

        def south_flux(j):
            return [scales[j] * (v[j - 1, p] + v[j, p]) * (h[j - 1, p] + h[j, p]) for p in range(parts)]

        def finish(j, tiles, moved):
            dst[0][j, 0] = tiles[0] + moved
            for p in range(1, parts):
                dst[0][j, p] = tiles[p]

        for j in range(lo - 2, lo + 1):
            column(j)
        flux_north = south_flux(lo)
        pending = []
        for j in range(lo, hi):
            column(j + 1)
            hj, uj, vj, gj = ([f[j, p] for p in range(parts)] for f in (h, u, v, geo))
            hj.append(after(hj[0]))
            uj.append(after(uj[0]))
            gj = [before(gj[-1]), *gj, after(gj[0])]
            flux = south_flux(j + 1)
            east = [(0.25 * time_step) * (uj[p] + uj[p + 1]) * (hj[p] + hj[p + 1]) for p in range(parts)]
            tiles = [hj[0] - (east[0] + (flux[0] - flux_north[0]))]
            tiles += [hj[p] - ((east[p] - east[p - 1]) + (flux[p] - flux_north[p])) for p in range(1, parts)]
            pending.append((j, tiles, before(east[-1])))
            for p in range(parts):
                east_ref[step, j, p] = east[p]
                south_ref[step, j, p] = flux_north[p]
                slope_x = gj[p + 2] - gj[p]
                slope_y = geo[j + 1, p] - geo[j - 1, p]
                dst[1][j, p] = uj[p] + time_step * (coriolis * vj[p] - 0.5 * slope_x)
                dst[2][j, p] = vj[p] - time_step * (coriolis * uj[p] + 0.5 * slope_y)
            flux_north = flux
            if len(pending) > DELAY:
                finish(*pending.pop(0))
        for one in pending:
            finish(*one)
        for p in range(parts):
            south_ref[step, hi, p] = flux_north[p]
        column(hi + 1)
        src, dst = dst, src
    block = h_out.shape[0]
    for out, field in zip((h_out, u_out, v_out), src):
        for k in range(block):
            mine = pl.ds(place[0] * block + k, 1)
            for q in range(0, rows, 8):
                tiles = restore([
                    jnp.concatenate([field[halo + q + i, p, mine, :] for i in range(8)], 0) for p in range(parts)])
                for p, tile in enumerate(tiles):
                    out[k, q:q + 8, p * LANES:(p + 1) * LANES] = tile


def tracer_kernel(place, counts, flags, *refs, first, lead):
    step_id = pl.program_id(0)
    if lead:
        planes, (north, top, bottom, south, out_ref), refs = refs[:6], refs[6:11], refs[11:]
        states, kept, refs = refs[:3], refs[3:6], refs[6:]
    else:
        kept, (north, top, bottom, south, _, out_ref), refs = refs[:3], refs[3:9], refs[9:]
    (cur, even, odd), fluxes, done, work = refs[:3], refs[3:6], refs[6], refs[7:]
    pairs = zip(fluxes, kept) if lead else zip(kept, fluxes)
    copies = [pltpu.make_async_copy(a, b, done.at[i]) for i, (a, b) in enumerate(pairs)]

    @pl.when(step_id == 0)
    def _():
        if lead:
            run_dynamics(place, *planes, *states, *fluxes, *work)
        for copy in copies:
            copy.start()
        if not lead:
            for copy in copies:
                copy.wait()

    inv_ref, east_ref, south_ref = fluxes
    batch = north.shape[0]
    parts = north.shape[2]
    halo = north.shape[1]
    half = top.shape[1]
    rows = 2 * half
    total = rows + 2 * halo
    group = place[0]
    start = jnp.int32(0)
    for g in range(counts.shape[0]):
        start = start + jnp.where(g < group, counts[g], 0)

    def entry(t, j):
        for source, base in ((south, halo + rows), (bottom, halo + half), (top, halo), (north, 0)):
            if j >= base:
                return [source[t, j - base, p] for p in range(parts)]

    def run(t, limited):
        def spread(buffer, j, tiles):
            for p in range(parts):
                buffer[j, p + 1] = tiles[p]
            buffer[j, 0] = before(tiles[-1])
            buffer[j, parts + 1] = after(tiles[0])
            buffer[j, parts + 2] = after(tiles[1])

        for j in range(total):
            spread(even, j, [t * inv_ref[0, j, p] for p, t in enumerate(entry(t, j))])

        def face(a2, a, b, b2, bounds):
            raw = 7.0 * (a + b) - (a2 + b2)
            if limited:
                raw = jnp.minimum(jnp.maximum(raw, jnp.minimum(*bounds)), jnp.maximum(*bounds))
            return raw

        def scaled(tiles):
            return [12.0 * t for t in tiles] if limited else [None] * len(tiles)

        src, dst = even, odd
        for step in range(STEPS):
            lo, hi = 2 * (step + 1), total - 2 * (step + 1)

            def south_terms(j, near, bounds):
                return [south_ref[step, j, p] * face(*(t[p] for t in near), tuple(t[p] for t in bounds))
                        for p in range(parts)]

            def load(j):
                return [src[j, p + 1] for p in range(parts)]

            def finish(j, tiles, moved):
                tiles = [tiles[0] + moved, *tiles[1:]]
                if step + 1 == STEPS:
                    tiles = restore(tiles)
                for p in range(parts):
                    cur[j, p] = tiles[p]
                if step + 1 < STEPS:
                    spread(dst, j, [t * inv_ref[step + 1, j, p] for p, t in enumerate(tiles)])

            near = [load(lo - 2 + b) for b in range(4)]
            bound = [scaled(near[1]), scaled(near[2])]
            term = south_terms(lo, near, bound)
            pending = []
            for j in range(lo, hi):
                near = [*near[1:], load(j + 2)]
                bound = [bound[1], scaled(near[2])]
                wide = [src[j, 0], *near[1], src[j, parts + 1], src[j, parts + 2]]
                limit = bound[0] + scaled([wide[parts + 1]])
                east = [east_ref[step, j, p] * face(*wide[p:p + 4], (limit[p], limit[p + 1]))
                        for p in range(parts)]
                moved = before(east[-1])
                following = south_terms(j + 1, near, bound)
                mass = entry(t, j) if step == 0 else [cur[j, p] for p in range(parts)]
                tiles = [mass[0] - (east[0] + (following[0] - term[0]))]
                tiles += [mass[p] - ((east[p] - east[p - 1]) + (following[p] - term[p])) for p in range(1, parts)]
                term = following
                pending.append((j, tiles, moved))
                if len(pending) > DELAY:
                    finish(*pending.pop(0))
            for one in pending:
                finish(*one)
            src, dst = dst, src
        for q in range(0, rows, 8):
            base = halo + q
            for p in range(parts):
                out_ref[t, :, q:q + 8, p * LANES:(p + 1) * LANES] = jnp.swapaxes(cur[base:base + 8, p], 0, 1)

    def one(t, carry):
        slot = step_id * batch + t + first
        live = slot < counts[group]
        flag = flags[jnp.minimum(start + slot, flags.shape[0] - 1)]

        @pl.when(live & (flag > 0))
        def _():
            run(t, True)

        @pl.when(live & (flag <= 0))
        def _():
            run(t, False)

        @pl.when(jnp.logical_not(live))
        def _():
            out_ref[t] = jnp.zeros(out_ref.shape[1:], jnp.float32)

        return carry

    lax.fori_loop(0, batch, one, 0)

    if lead:
        @pl.when(step_id == pl.num_programs(0) - 1)
        def _():
            for copy in copies:
                copy.wait()


def whole_block(shape):
    return pl.BlockSpec(shape, lambda *_: (0,) * len(shape))


def run_arrange(mass, first, count):
    _, levels, rows, columns = mass.shape
    batch = next(b for b in range(4, 0, -1) if math.gcd(count, first) % b == 0)
    half = jax.ShapeDtypeStruct((count, rows // 2, columns // LANES, levels, LANES), jnp.float32)
    return pl.pallas_call(
        arrange_kernel,
        grid=(count // batch,),
        in_specs=[pl.BlockSpec((batch, levels, rows, columns), lambda i: (i + first // batch, 0, 0, 0))],
        out_specs=[pl.BlockSpec((batch, *half.shape[1:]), lambda i: (i, 0, 0, 0, 0))] * 2,
        out_shape=[half] * 2,
        name="arrange",
    )(mass)


def run_tracers(place, counts, flags, blocks, planes, kept, earlier, first, out_shape):
    lead = planes is not None
    count, half, parts, levels, lanes = blocks[0].shape
    rows, columns = 2 * half, parts * lanes
    total = rows + 2 * HALO
    tiles = (total, parts, levels, lanes)
    wide = (total, parts + 3, levels, lanes)
    anywhere = pl.BlockSpec(memory_space=pl.ANY)
    batch = math.gcd(BATCH, count, first)
    block_specs = [pl.BlockSpec((batch, *b.shape[1:]), lambda i, *_: (i, 0, 0, 0, 0)) for b in blocks]
    out_specs = [pl.BlockSpec((batch, *out_shape[1:]), lambda i, *_: (i + first // batch, 0, 0, 0))]
    out_types = [jax.ShapeDtypeStruct(out_shape, jnp.float32)]
    scratch = [tiles, wide, wide] + [(STEPS, *tiles)] * 3
    scratch = [pltpu.VMEM(s, jnp.float32) for s in scratch] + [pltpu.SemaphoreType.DMA((3,))]
    aliases = {}
    if lead:
        state = (1, rows, columns)
        operands = [*planes, *blocks]
        in_specs = [whole_block(p.shape) for p in planes] + block_specs
        out_specs += [whole_block(state)] * 3 + [anywhere] * 3
        out_types += [jax.ShapeDtypeStruct(state, jnp.float32)] * 3
        out_types += [jax.ShapeDtypeStruct((STEPS, *tiles), jnp.float32)] * 3
        work = [tiles] * 7 + [(3, levels, total, columns)]
        scratch += [pltpu.VMEM(s, jnp.float32) for s in work]
    else:
        operands = [*kept, *blocks, earlier]
        in_specs = [anywhere] * 3 + block_specs + [anywhere]
        aliases = {2 + len(operands): 0}
    return pl.pallas_call(
        functools.partial(tracer_kernel, first=first, lead=lead),
        grid_spec=pltpu.PrefetchScalarGridSpec(
            num_scalar_prefetch=3,
            grid=(count // batch,),
            in_specs=in_specs,
            out_specs=out_specs,
            scratch_shapes=scratch,
        ),
        out_shape=out_types,
        input_output_aliases=aliases,
        compiler_params=pltpu.CompilerParams(vmem_limit_bytes=52 << 20),
        name="tracers",
    )(place, counts, flags, *operands)


def on_device(tracer_mass, layer_mass, zonal_wind, merid_wind, group_counts, limiter_flags):
    n_comp = lax.axis_size("comp")
    n_band = lax.axis_size("band")
    slots, levels, rows, _ = tracer_mass.shape
    level_block = layer_mass.shape[0]
    assert rows == 2 * HALO and levels == 8
    place = jnp.stack([
        lax.axis_index("comp"), lax.axis_index("band") * rows, jnp.int32(rows * n_band)
    ]).astype(jnp.int32)
    majors = n_comp // 2
    assert level_block == 1 and n_comp == levels and levels % 2 == 0

    def swap_minor(block):
        return lax.ppermute(block, "comp", [(i, i ^ 1) for i in range(n_comp)])

    state = jnp.concatenate([layer_mass, zonal_wind, merid_wind], 0)
    received = []
    for d in range(1, majors):
        received.append(lax.ppermute(state, "comp", [(i, (i + 2 * d) % n_comp) for i in range(n_comp)]))
    near = lax.optimization_barrier(jnp.concatenate(received, 0))
    far_state = swap_minor(state)
    far = swap_minor(near)
    pieces = (state, near, far_state, far)
    from_north = band_shift(jnp.concatenate([x[:, rows - HALO:] for x in pieces], 0), 1)
    from_south = band_shift(jnp.concatenate([x[:, :HALO] for x in pieces], 0), -1)
    chunk = (3 * slots) // 8
    blocks = []
    for first, count in ((0, chunk), (chunk, slots - chunk)):
        top, bottom = run_arrange(tracer_mass, first, count)
        north = band_shift(bottom, 1)
        south = band_shift(top, -1)
        blocks.append((north, top, bottom, south))
    planes = (*pieces, from_north, from_south)
    earlier, height, zonal, merid, *kept = run_tracers(
        place, group_counts, limiter_flags, blocks[0], planes, None, None, 0, tracer_mass.shape)
    tracers, = run_tracers(
        place, group_counts, limiter_flags, blocks[1], None, kept, earlier, chunk, tracer_mass.shape)
    return tracers, height, zonal, merid


def solution(mesh):
    placed = (
        P("comp", None, "band", None),
        P("comp", "band", None),
        P("comp", "band", None),
        P("comp", "band", None),
        P(),
        P(),
    )
    return jax.shard_map(
        on_device,
        mesh=mesh,
        in_specs=placed,
        out_specs=placed[:4],
        check_vma=False,
    )
```

```python
import functools
import math

import jax
import jax.numpy as jnp
from jax import lax
from jax.experimental import pallas as pl
from jax.experimental.pallas import tpu as pltpu
from jax.sharding import PartitionSpec as P


STEPS = 4
HALO = 2 * STEPS

time_step = 0.1
gravity = 0.25
coriolis = 0.5
mass_floor = 0.5


LANES = 128
DELAY = 6
BATCH = 1


def band_shift(block, offset):
    count = lax.axis_size("band")
    pairs = [(i, i + offset) for i in range(count) if 0 <= i + offset < count]
    return lax.ppermute(block, "band", pairs)


def lane_index(shape):
    return lax.broadcasted_iota(jnp.int32, shape, len(shape) - 1)


def swap_bits(tiles):
    tiles = list(tiles)
    lane = lane_index(tiles[0].shape)
    bit = 1
    while bit < len(tiles):
        keep = (lane & bit) == 0
        for a in range(len(tiles)):
            if not a & bit:
                b = a | bit
                first, second = tiles[a], tiles[b]
                axis = first.ndim - 1
                tiles[a] = jnp.where(keep, first, pltpu.roll(second, bit, axis))
                tiles[b] = jnp.where(keep, pltpu.roll(first, LANES - bit, axis), second)
        bit *= 2
    return tiles


def lane_order(shape, parts, inverse):
    lane = lane_index(shape)
    few, many = (parts, LANES // parts) if inverse else (LANES // parts, parts)
    return (lane & (few - 1)) * many + (lane >> (few.bit_length() - 1))


def take_lanes(tile, index):
    return jnp.take_along_axis(tile, index, axis=1, mode="promise_in_bounds")


def interleave(tiles):
    order = lane_order(tiles[0].shape[-2:], len(tiles), False)
    return [take_each(t, order) for t in swap_bits(tiles)]


def restore(tiles):
    order = lane_order(tiles[0].shape[-2:], len(tiles), True)
    return swap_bits([take_each(t, order) for t in tiles])


def take_each(tile, order):
    if tile.ndim == 2:
        return take_lanes(tile, order)
    return jnp.stack([take_lanes(tile[i], order) for i in range(tile.shape[0])])


def after(tile):
    return pltpu.roll(tile, LANES - 1, 1)


def before(tile):
    return pltpu.roll(tile, 1, 1)


def plane_order(levels):
    return [(field, d, flip) for flip in range(2) for d in range(levels // 2) for field in range(3)]


def source_level(comp, levels, major, flip):
    majors = levels // 2
    at = (comp >> 1) - major
    return jnp.where(at < 0, at + majors, at) * 2 + ((comp & 1) ^ flip)


def split_row(row):
    return [row[..., p * LANES:(p + 1) * LANES] for p in range(row.shape[-1] // LANES)]


def arrange_kernel(mass, top, bottom):
    rows = mass.shape[2]
    half = rows // 2

    for t in range(mass.shape[0]):
        for out, base in ((top, 0), (bottom, half)):
            for q in range(0, half, 8):
                block = jnp.swapaxes(mass[t, :, base + q:base + q + 8], 0, 1)
                for p, tile in enumerate(interleave(split_row(block))):
                    out[t, q:q + 8, p] = tile


def run_dynamics(place, state, near, far_state, far, north, south, h_out, u_out, v_out, inv_ref, east_ref, south_ref,
                 h0, u0, v0, h1, u1, v1, geo, stage):
    planes, rows, columns = north.shape[0], *near.shape[1:]
    parts = columns // LANES
    halo = north.shape[1]
    total = rows + 2 * halo
    levels = planes // 3
    sources = [(piece, i) for piece in (state, near, far_state, far) for i in range(piece.shape[0])]
    for plane, (field, major, flip) in enumerate(plane_order(levels)):
        level = source_level(place[0], levels, major, flip)
        own = sources[plane][0][sources[plane][1]]
        for block, base in ((north[plane], 0), (own, halo), (south[plane], halo + rows)):
            stage[field, level, base:base + block.shape[0]] = block
    for field, dst in enumerate((h0, u0, v0)):
        for q in range(0, total, 8):
            block = jnp.swapaxes(stage[field, :, q:q + 8], 0, 1)
            for p, tile in enumerate(interleave(split_row(block))):
                dst[q:q + 8, p] = tile
    first_face = place[1] - halo
    scales = [jnp.where((first_face + j > 0) & (first_face + j < place[2]), 0.25 * time_step, 0.0)
              for j in range(total)]
    level = lax.broadcasted_iota(jnp.int32, (levels, LANES), 0)
    src, dst = (h0, u0, v0), (h1, u1, v1)
    for step in range(STEPS):
        h, u, v = src
        lo, hi = 2 * (step + 1), total - 2 * (step + 1)

        def column(j):
            for p in range(parts):
                hp = h[j, p]
                acc = hp
                span = 1
                while span < levels:
                    moved = pltpu.roll(acc, levels - span, 0)
                    acc = acc + jnp.where(level < levels - span, moved, 0.0)
                    span *= 2
                geo[j, p] = gravity * acc
                inv_ref[step, j, p] = (1.0 / 12.0) / jnp.maximum(hp, mass_floor)

        def south_flux(j):
            return [scales[j] * (v[j - 1, p] + v[j, p]) * (h[j - 1, p] + h[j, p]) for p in range(parts)]

        def finish(j, tiles, moved):
            dst[0][j, 0] = tiles[0] + moved
            for p in range(1, parts):
                dst[0][j, p] = tiles[p]

        for j in range(lo - 2, lo + 1):
            column(j)
        flux_north = south_flux(lo)
        pending = []
        for j in range(lo, hi):
            column(j + 1)
            hj, uj, vj, gj = ([f[j, p] for p in range(parts)] for f in (h, u, v, geo))
            hj.append(after(hj[0]))
            uj.append(after(uj[0]))
            gj = [before(gj[-1]), *gj, after(gj[0])]
            flux = south_flux(j + 1)
            east = [(0.25 * time_step) * (uj[p] + uj[p + 1]) * (hj[p] + hj[p + 1]) for p in range(parts)]
            tiles = [hj[0] - (east[0] + (flux[0] - flux_north[0]))]
            tiles += [hj[p] - ((east[p] - east[p - 1]) + (flux[p] - flux_north[p])) for p in range(1, parts)]
            pending.append((j, tiles, before(east[-1])))
            for p in range(parts):
                east_ref[step, j, p] = east[p]
                south_ref[step, j, p] = flux_north[p]
                slope_x = gj[p + 2] - gj[p]
                slope_y = geo[j + 1, p] - geo[j - 1, p]
                dst[1][j, p] = uj[p] + time_step * (coriolis * vj[p] - 0.5 * slope_x)
                dst[2][j, p] = vj[p] - time_step * (coriolis * uj[p] + 0.5 * slope_y)
            flux_north = flux
            if len(pending) > DELAY:
                finish(*pending.pop(0))
        for one in pending:
            finish(*one)
        for p in range(parts):
            south_ref[step, hi, p] = flux_north[p]
        column(hi + 1)
        src, dst = dst, src
    block = h_out.shape[0]
    for out, field in zip((h_out, u_out, v_out), src):
        for k in range(block):
            mine = pl.ds(place[0] * block + k, 1)
            for q in range(0, rows, 8):
                tiles = restore([
                    jnp.concatenate([field[halo + q + i, p, mine, :] for i in range(8)], 0) for p in range(parts)])
                for p, tile in enumerate(tiles):
                    out[k, q:q + 8, p * LANES:(p + 1) * LANES] = tile


def tracer_kernel(place, counts, flags, *refs, first, lead):
    step_id = pl.program_id(0)
    if lead:
        planes, (north, top, bottom, south, out_ref), refs = refs[:6], refs[6:11], refs[11:]
        states, kept, refs = refs[:3], refs[3:6], refs[6:]
    else:
        kept, (north, top, bottom, south, _, out_ref), refs = refs[:3], refs[3:9], refs[9:]
    (cur, even, odd), fluxes, done, work = refs[:3], refs[3:6], refs[6], refs[7:]
    pairs = zip(fluxes, kept) if lead else zip(kept, fluxes)
    copies = [pltpu.make_async_copy(a, b, done.at[i]) for i, (a, b) in enumerate(pairs)]

    @pl.when(step_id == 0)
    def _():
        if lead:
            run_dynamics(place, *planes, *states, *fluxes, *work)
        for copy in copies:
            copy.start()
        if not lead:
            for copy in copies:
                copy.wait()

    inv_ref, east_ref, south_ref = fluxes
    batch = north.shape[0]
    parts = north.shape[2]
    halo = north.shape[1]
    half = top.shape[1]
    rows = 2 * half
    total = rows + 2 * halo
    group = place[0]
    start = jnp.int32(0)
    for g in range(counts.shape[0]):
        start = start + jnp.where(g < group, counts[g], 0)

    def entry(t, j):
        for source, base in ((south, halo + rows), (bottom, halo + half), (top, halo), (north, 0)):
            if j >= base:
                return [source[t, j - base, p] for p in range(parts)]

    def run(t, limited):
        def spread(buffer, j, tiles):
            for p in range(parts):
                buffer[j, p + 1] = tiles[p]
            buffer[j, 0] = before(tiles[-1])
            buffer[j, parts + 1] = after(tiles[0])
            buffer[j, parts + 2] = after(tiles[1])

        for j in range(total):
            spread(even, j, [t * inv_ref[0, j, p] for p, t in enumerate(entry(t, j))])

        def face(a2, a, b, b2, bounds):
            raw = 7.0 * (a + b) - (a2 + b2)
            if limited:
                raw = jnp.minimum(jnp.maximum(raw, jnp.minimum(*bounds)), jnp.maximum(*bounds))
            return raw

        def scaled(tiles):
            return [12.0 * t for t in tiles] if limited else [None] * len(tiles)

        src, dst = even, odd
        for step in range(STEPS):
            lo, hi = 2 * (step + 1), total - 2 * (step + 1)

            def south_terms(j, near, bounds):
                return [south_ref[step, j, p] * face(*(t[p] for t in near), tuple(t[p] for t in bounds))
                        for p in range(parts)]

            def load(j):
                return [src[j, p + 1] for p in range(parts)]

            def finish(j, tiles, moved):
                tiles = [tiles[0] + moved, *tiles[1:]]
                if step + 1 == STEPS:
                    tiles = restore(tiles)
                for p in range(parts):
                    cur[j, p] = tiles[p]
                if step + 1 < STEPS:
                    spread(dst, j, [t * inv_ref[step + 1, j, p] for p, t in enumerate(tiles)])

            near = [load(lo - 2 + b) for b in range(4)]
            bound = [scaled(near[1]), scaled(near[2])]
            term = south_terms(lo, near, bound)
            pending = []
            for j in range(lo, hi):
                near = [*near[1:], load(j + 2)]
                bound = [bound[1], scaled(near[2])]
                wide = [src[j, 0], *near[1], src[j, parts + 1], src[j, parts + 2]]
                limit = bound[0] + scaled([wide[parts + 1]])
                east = [east_ref[step, j, p] * face(*wide[p:p + 4], (limit[p], limit[p + 1]))
                        for p in range(parts)]
                moved = before(east[-1])
                following = south_terms(j + 1, near, bound)
                mass = entry(t, j) if step == 0 else [cur[j, p] for p in range(parts)]
                tiles = [mass[0] - (east[0] + (following[0] - term[0]))]
                tiles += [mass[p] - ((east[p] - east[p - 1]) + (following[p] - term[p])) for p in range(1, parts)]
                term = following
                pending.append((j, tiles, moved))
                if len(pending) > DELAY:
                    finish(*pending.pop(0))
            for one in pending:
                finish(*one)
            src, dst = dst, src
        for q in range(0, rows, 8):
            base = halo + q
            for p in range(parts):
                out_ref[t, :, q:q + 8, p * LANES:(p + 1) * LANES] = jnp.swapaxes(cur[base:base + 8, p], 0, 1)

    def one(t, carry):
        slot = step_id * batch + t + first
        live = slot < counts[group]
        flag = flags[jnp.minimum(start + slot, flags.shape[0] - 1)]

        @pl.when(live & (flag > 0))
        def _():
            run(t, True)

        @pl.when(live & (flag <= 0))
        def _():
            run(t, False)

        @pl.when(jnp.logical_not(live))
        def _():
            out_ref[t] = jnp.zeros(out_ref.shape[1:], jnp.float32)

        return carry

    lax.fori_loop(0, batch, one, 0)

    if lead:
        @pl.when(step_id == pl.num_programs(0) - 1)
        def _():
            for copy in copies:
                copy.wait()


def whole_block(shape):
    return pl.BlockSpec(shape, lambda *_: (0,) * len(shape))


def run_arrange(mass, first, count):
    _, levels, rows, columns = mass.shape
    batch = next(b for b in range(4, 0, -1) if math.gcd(count, first) % b == 0)
    half = jax.ShapeDtypeStruct((count, rows // 2, columns // LANES, levels, LANES), jnp.float32)
    return pl.pallas_call(
        arrange_kernel,
        grid=(count // batch,),
        in_specs=[pl.BlockSpec((batch, levels, rows, columns), lambda i: (i + first // batch, 0, 0, 0))],
        out_specs=[pl.BlockSpec((batch, *half.shape[1:]), lambda i: (i, 0, 0, 0, 0))] * 2,
        out_shape=[half] * 2,
        name="arrange",
    )(mass)


def run_tracers(place, counts, flags, blocks, planes, kept, earlier, first, out_shape):
    lead = planes is not None
    count, half, parts, levels, lanes = blocks[0].shape
    rows, columns = 2 * half, parts * lanes
    total = rows + 2 * HALO
    tiles = (total, parts, levels, lanes)
    wide = (total, parts + 3, levels, lanes)
    anywhere = pl.BlockSpec(memory_space=pl.ANY)
    batch = math.gcd(BATCH, count, first)
    block_specs = [pl.BlockSpec((batch, *b.shape[1:]), lambda i, *_: (i, 0, 0, 0, 0)) for b in blocks]
    out_specs = [pl.BlockSpec((batch, *out_shape[1:]), lambda i, *_: (i + first // batch, 0, 0, 0))]
    out_types = [jax.ShapeDtypeStruct(out_shape, jnp.float32)]
    scratch = [tiles, wide, wide] + [(STEPS, *tiles)] * 3
    scratch = [pltpu.VMEM(s, jnp.float32) for s in scratch] + [pltpu.SemaphoreType.DMA((3,))]
    aliases = {}
    if lead:
        state = (1, rows, columns)
        operands = [*planes, *blocks]
        in_specs = [whole_block(p.shape) for p in planes] + block_specs
        out_specs += [whole_block(state)] * 3 + [anywhere] * 3
        out_types += [jax.ShapeDtypeStruct(state, jnp.float32)] * 3
        out_types += [jax.ShapeDtypeStruct((STEPS, *tiles), jnp.float32)] * 3
        work = [tiles] * 7 + [(3, levels, total, columns)]
        scratch += [pltpu.VMEM(s, jnp.float32) for s in work]
    else:
        operands = [*kept, *blocks, earlier]
        in_specs = [anywhere] * 3 + block_specs + [anywhere]
        aliases = {2 + len(operands): 0}
    return pl.pallas_call(
        functools.partial(tracer_kernel, first=first, lead=lead),
        grid_spec=pltpu.PrefetchScalarGridSpec(
            num_scalar_prefetch=3,
            grid=(count // batch,),
            in_specs=in_specs,
            out_specs=out_specs,
            scratch_shapes=scratch,
        ),
        out_shape=out_types,
        input_output_aliases=aliases,
        compiler_params=pltpu.CompilerParams(vmem_limit_bytes=52 << 20),
        name="tracers",
    )(place, counts, flags, *operands)


def on_device(tracer_mass, layer_mass, zonal_wind, merid_wind, group_counts, limiter_flags):
    n_comp = lax.axis_size("comp")
    n_band = lax.axis_size("band")
    slots, levels, rows, columns = tracer_mass.shape
    level_block = layer_mass.shape[0]
    assert rows == 2 * HALO and levels == 8
    place = jnp.stack([
        lax.axis_index("comp"), lax.axis_index("band") * rows, jnp.int32(rows * n_band)
    ]).astype(jnp.int32)
    majors = n_comp // 2
    assert level_block == 1 and n_comp == levels and levels % 2 == 0

    def swap_minor(block):
        return lax.ppermute(block, "comp", [(i, i ^ 1) for i in range(n_comp)])

    field = lax.broadcasted_iota(jnp.int32, (3, rows, columns), 0)
    state = jnp.where(field == 0, layer_mass, jnp.where(field == 1, zonal_wind, merid_wind))
    received = []
    for d in range(1, majors):
        received.append(lax.ppermute(state, "comp", [(i, (i + 2 * d) % n_comp) for i in range(n_comp)]))
    near = lax.optimization_barrier(jnp.concatenate(received, 0))
    far_state = swap_minor(state)
    far = swap_minor(near)
    pieces = (state, near, far_state, far)
    from_north = band_shift(jnp.concatenate([x[:, rows - HALO:] for x in pieces], 0), 1)
    from_south = band_shift(jnp.concatenate([x[:, :HALO] for x in pieces], 0), -1)
    chunk = (3 * slots) // 8
    blocks = []
    for first, count in ((0, chunk), (chunk, slots - chunk)):
        top, bottom = run_arrange(tracer_mass, first, count)
        north = band_shift(bottom, 1)
        south = band_shift(top, -1)
        blocks.append((north, top, bottom, south))
    planes = (*pieces, from_north, from_south)
    earlier, height, zonal, merid, *kept = run_tracers(
        place, group_counts, limiter_flags, blocks[0], planes, None, None, 0, tracer_mass.shape)
    tracers, = run_tracers(
        place, group_counts, limiter_flags, blocks[1], None, kept, earlier, chunk, tracer_mass.shape)
    return tracers, height, zonal, merid


def solution(mesh):
    placed = (
        P("comp", None, "band", None),
        P("comp", "band", None),
        P("comp", "band", None),
        P("comp", "band", None),
        P(),
        P(),
    )
    return jax.shard_map(
        on_device,
        mesh=mesh,
        in_specs=placed,
        out_specs=placed[:4],
        check_vma=False,
    )
```
